512 devices in a mesh: tile: 128 (over x, z_hi, y, core), depth: 4 (over z_lo).
Axes of the slice: x: 4, y: 8, z: 8 (z_hi: 2, z_lo: 4; z = z_hi * 4 + z_lo), core: 2. Of those that a mesh axis runs over, the one named last changes fastest.
Arguments:
- transmission: float32 [2, 4, 16384, 512], P(None, 'depth', 'tile'), may hold values from -1.2 to 1.2, as said below
- probe_wave: float32 [2, 128, 128], replicated, may hold values from -6 to 6
- fresnel_phase: float32 [128, 128], replicated, may hold values from -3.140625 to 3.140625
- measured: float32 [512, 128, 128], P('tile'), may hold values from 0.1 to 4
- positions: int32 [512, 2], P('tile'), may hold values from 0 to 16383, as said below
- extents: int32 [128, 2], P('tile'), may hold values from 32 to 64
Outputs:
- object_grad: float32 [2, 4, 16384, 512], P(None, 'depth', 'tile')
The draws below stay inside these ranges and needn't reach their ends.
Inputs may be any that keep to these rules, and one draw needn't show every extreme that they name: `transmission`: real and imaginary parts of a pixel form a complex number of modulus 0.7 to 1.2. `positions`: probe p belongs to tile t = p // 4. Its first row r satisfies ((r - 128 t + 64) mod 16384) - 64 between -64 and 64, both ends reached in every draw; its first column lies between 0 and 384.
All inputs are finite; a program needn't handle non-finite values.
Results may differ from the reference program's by a relative error of at most 0.025.
Values may be sent and summed in bfloat16 or wider, within the bound.
A program may use at most 64 MiB of HBM per device.

```python
import math
import jax
import jax.numpy as jnp
from jax import lax

W = 128
BAND = 64
PPT = 4
SL = 1
STRIP = 128
OW = 512
NROWS = 16384
PROBES = 512
SLICES = 4
N_TILE = 128


def draw_transmission(key, part):
    key_amp, key_phase = jax.random.split(jax.random.fold_in(key, 11))
    shape = (SLICES, NROWS, OW)
    amplitude = jax.random.uniform(key_amp, shape, jnp.float32, 0.7, 1.1)
    phase = jax.random.uniform(key_phase, shape, jnp.float32, -1.0, 1.0)
    return jnp.stack([amplitude * jnp.cos(phase), amplitude * jnp.sin(phase)]).astype(jnp.float32)


def draw_positions(key, part):
    key_rows, key_cols, key_first, key_second = jax.random.split(jax.random.fold_in(key, 23), 4)
    probe_ids = jnp.arange(PROBES, dtype=jnp.int32)
    tile_ids = probe_ids // PPT
    offset = jax.random.randint(key_rows, (PROBES,), -BAND, STRIP + BAND - W + 1, dtype=jnp.int32)
    upper_tile = jax.random.randint(key_first, (), 0, N_TILE, dtype=jnp.int32)
    lower_tile = jax.random.randint(key_second, (), 0, N_TILE, dtype=jnp.int32)
    offset = jnp.where(probe_ids == upper_tile * PPT, -BAND, offset)
    offset = jnp.where(probe_ids == lower_tile * PPT + 1, STRIP + BAND - W, offset)
    rows = (tile_ids * STRIP + offset) % NROWS
    columns = jax.random.randint(key_cols, (PROBES,), 0, OW - W + 1, dtype=jnp.int32)
    return jnp.stack([rows, columns], axis=1).astype(jnp.int32)


def set_ends(drawn, rng, least, largest):
    dims = drawn.shape
    place = [jax.random.randint(jax.random.fold_in(rng, axis), (), 0, dims[axis]) for axis in range(len(dims))]
    drawn = drawn.at[tuple(place)].set(least)
    longest = dims.index(max(dims))
    place[longest] = (place[longest] + 1) % dims[longest]
    return drawn.at[tuple(place)].set(largest)


def levels(stream_key, extent, shards, low, top_value):
    def one(dim, parts):
        heights = jax.random.uniform(jax.random.fold_in(jax.random.fold_in(stream_key, 6), dim), (parts,), jnp.float32, low / len(shards), top_value / len(shards))
        return jnp.repeat(jnp.exp(heights), extent[dim] // parts).reshape((-1,) + (1,) * (len(extent) - dim - 1))

    loudness = one(*shards[0])
    for cut in shards[1:]:
        loudness = loudness * one(*cut)
    return loudness


def normal_values(rng, shape, deviation, most, kind=jnp.bfloat16):
    return jnp.clip(deviation * jax.random.normal(rng, shape, jnp.float32), -most, most).astype(kind)


def setup_inputs(seed: int = 0) -> dict:
    arg_keys = jax.random.split(jax.random.key(seed), 7)
    transmission = draw_transmission(jax.random.fold_in(arg_keys[6], 71), 0)
    probe_wave = normal_values(arg_keys[1], (2, W, W), 1.0, 6.0, jnp.float32)
    fresnel_phase = jnp.clip(jax.random.uniform(arg_keys[2], (W, W), jnp.float32, -3.140625, 3.140625), -3.140625, 3.140625)
    measured = jnp.clip(jnp.exp(math.log(4.0) - 3.6888794 * jax.random.uniform(arg_keys[3], (PROBES, W, W), jnp.float32) ** levels(arg_keys[3], (PROBES, W, W), ((0, 128),), -0.2, 0.2)), 0.1, 4.0)
    positions = draw_positions(jax.random.fold_in(arg_keys[6], 71), 0)
    extents = set_ends(jax.random.randint(arg_keys[5], (N_TILE, 2), BAND // 2, BAND + 1), jax.random.fold_in(arg_keys[5], 1), BAND // 2, BAND).astype(jnp.int32)
    return dict(transmission=transmission, probe_wave=probe_wave, fresnel_phase=fresnel_phase, measured=measured, positions=positions, extents=extents)


HIGHEST = lax.Precision.HIGHEST

def tables(length):
    indices = jnp.arange(length, dtype=jnp.int32)
    product = indices[:, None] * indices[None, :] % length
    angles = product.astype(jnp.float32) * (2.0 * math.pi / length)
    factor = 1.0 / math.sqrt(length)
    return (jnp.cos(angles) * factor, jnp.sin(angles) * factor)

def operators(length):
    cosine, sine_table = tables(length)

    def build_pair(direction):
        left_side = jnp.stack([jnp.stack([cosine, direction * sine_table]), jnp.stack([-direction * sine_table, cosine])])
        right_side = jnp.stack([jnp.stack([cosine, -direction * sine_table]), jnp.stack([direction * sine_table, cosine])])
        return (left_side, right_side)
    return (build_pair(1.0), build_pair(-1.0))

def transform(real_part, imag_part, matrices):
    stacked = jnp.stack([real_part, imag_part])
    halfway = jnp.einsum('xyab,ypbc->xpac', matrices[0], stacked, precision=HIGHEST)
    finished = jnp.einsum('ypab,yxbc->xpac', halfway, matrices[1], precision=HIGHEST)
    return (finished[0], finished[1])

def propagate(real_part, imag_part, phase_cos, phase_sin, forward_mats, inverse_mats, conjugate):
    spec_real, spec_imag = transform(real_part, imag_part, forward_mats)
    turned_real = spec_real * phase_cos - conjugate * spec_imag * phase_sin
    turned_imag = spec_imag * phase_cos + conjugate * spec_real * phase_sin
    return transform(turned_real, turned_imag, inverse_mats)

def to_wire(values):
    return lax.optimization_barrier(values.astype(jnp.bfloat16)).astype(jnp.float32)

def reference(transmission, probe_wave, fresnel_phase, measured, positions, extents):
    forward_mats, inverse_mats = operators(W)
    phase_cos = jnp.cos(fresnel_phase)
    phase_sin = jnp.sin(fresnel_phase)
    row_first = positions[:, 0]
    col_first = positions[:, 1]
    probe_ids = jnp.arange(PROBES, dtype=jnp.int32)
    tile_ids = probe_ids // PPT
    offset = (row_first - tile_ids * STRIP + BAND) % NROWS - BAND
    lines = jnp.arange(W, dtype=jnp.int32)
    relative = offset[:, None] + lines[None, :]
    inside = (relative >= -extents[tile_ids, 0][:, None]) & (relative < STRIP + extents[tile_ids, 1][:, None])
    row_mask = inside.astype(jnp.float32)[:, :, None]
    wave_real = probe_wave[0][None] * row_mask
    wave_imag = probe_wave[1][None] * row_mask
    row_index = ((row_first[:, None] + lines[None, :]) % NROWS)[:, :, None]
    col_index = (col_first[:, None] + lines[None, :])[:, None, :]
    waves = []
    layers = []
    for slice_index in range(SLICES):
        layer_real = transmission[0, slice_index][row_index, col_index]
        layer_imag = transmission[1, slice_index][row_index, col_index]
        waves.append((wave_real, wave_imag))
        layers.append((layer_real, layer_imag))
        mixed_real = wave_real * layer_real - wave_imag * layer_imag
        mixed_imag = wave_real * layer_imag + wave_imag * layer_real
        wave_real, wave_imag = propagate(mixed_real, mixed_imag, phase_cos, phase_sin, forward_mats, inverse_mats, 1.0)
        if (slice_index + 1) % SL == 0 and slice_index + 1 < SLICES:
            wave_real = to_wire(wave_real)
            wave_imag = to_wire(wave_imag)
    far_real, far_imag = transform(wave_real, wave_imag, forward_mats)
    misfit = far_real * far_real + far_imag * far_imag - measured
    back_real, back_imag = transform(misfit * far_real, misfit * far_imag, inverse_mats)
    object_grad = jnp.zeros((2, SLICES, NROWS, OW), jnp.float32)
    for slice_index in reversed(range(SLICES)):
        adj_real, adj_imag = propagate(back_real, back_imag, phase_cos, phase_sin, forward_mats, inverse_mats, -1.0)
        held_real, held_imag = waves[slice_index]
        layer_real, layer_imag = layers[slice_index]
        term_real = held_real * adj_real + held_imag * adj_imag
        term_imag = held_real * adj_imag - held_imag * adj_real
        object_grad = object_grad.at[0, slice_index, row_index, col_index].add(term_real)
        object_grad = object_grad.at[1, slice_index, row_index, col_index].add(term_imag)
        back_real = layer_real * adj_real + layer_imag * adj_imag
        back_imag = layer_real * adj_imag - layer_imag * adj_real
        if slice_index % SL == 0 and slice_index > 0:
            back_real = to_wire(back_real)
            back_imag = to_wire(back_imag)
    return object_grad
```

```python
import math

import jax
import jax.numpy as jnp
import numpy as np
from jax import lax
from jax.experimental import pallas as pl
from jax.experimental.pallas import tpu as pltpu
from jax.sharding import PartitionSpec as P

BAND = 64
W = 128
STRIP = 128
OW = 512
BLOCKS = OW // W
DEPTH = 4
F32 = jnp.float32
BF16 = jnp.bfloat16
MESH = pl.DeviceIdType.MESH


def dft_matrices():
    index = np.arange(W)
    angles = (index[:, None] * index[None, :] % W) * (2.0 * math.pi / W)
    cosine = np.cos(angles) / math.sqrt(W)
    sine = np.sin(angles) / math.sqrt(W)
    a = np.block([[cosine, sine], [-sine, cosine]])
    b = a.T
    parts = []
    for m in (a, b):
        high = m.astype(BF16)
        low = (m - high.astype(np.float64)).astype(BF16)
        parts.append((high, low))
    right = np.stack([np.concatenate([h, l, h], axis=0) for h, l in (parts[1], parts[0])])
    left = np.stack([np.concatenate([h, l, h], axis=1) for h, l in (parts[0], parts[1])])
    return right, left


def kernel(
    tile_count,
    pos_ref, ext_ref, tr_hbm, probe_hbm, phase_hbm, meas_hbm, right_hbm, left_hbm,
    out_ref,
    tr, probe, phase, meas, right, left, gcos, gsin, waves,
    halo_send, halo, wsend, wrecv, gsend, grecv, band_send, band_recv,
    local_sem, hs, hr, ws, wr, gs, gr, bs, br,
):
    t = lax.axis_index("tile")
    me = lax.axis_index("depth")
    above = lax.rem(t + tile_count - 1, tile_count)
    below = lax.rem(t + 1, tile_count)
    peers = [lax.rem(me + j, DEPTH) for j in range(1, DEPTH)]

    barrier = pltpu.get_barrier_semaphore()
    pl.semaphore_signal(barrier, inc=1, device_id=(above, me), device_id_type=MESH)
    pl.semaphore_signal(barrier, inc=1, device_id=(below, me), device_id_type=MESH)
    for p in peers:
        pl.semaphore_signal(barrier, inc=1, device_id=(t, p), device_id_type=MESH)

    fetches = [
        pltpu.make_async_copy(tr_hbm.at[:, 0], tr, local_sem.at[0]),
        pltpu.make_async_copy(probe_hbm, probe, local_sem.at[1]),
        pltpu.make_async_copy(phase_hbm, phase, local_sem.at[2]),
        pltpu.make_async_copy(meas_hbm.at[me], meas, local_sem.at[3]),
        pltpu.make_async_copy(right_hbm, right, local_sem.at[4]),
        pltpu.make_async_copy(left_hbm, left, local_sem.at[5]),
    ]
    for f in fetches:
        f.start()

    def offset_of(p):
        rows = STRIP * tile_count
        return lax.rem(pos_ref[p, 0] - t * STRIP + (rows + BAND), rows) - BAND

    offs = [offset_of(p) for p in range(DEPTH)]
    cols = [pos_ref[p, 1] for p in range(DEPTH)]

    half_rows = lax.broadcasted_iota(jnp.int32, (BAND, W), 0)
    half_lanes = lax.broadcasted_iota(jnp.int32, (BAND, W), 1)

    def column_mask(p, m):
        position = half_lanes + m * W
        return (position >= cols[p]) & (position < cols[p] + W)

    def upward(p):
        return (half_rows * 0 + offs[p]) <= 0

    fetches[0].wait()
    for i in range(2):
        halo_send[i] = tr[:, i * BAND:(i + 1) * BAND, :].astype(BF16)

    for p in range(DEPTH):
        up = upward(p)
        for c in range(2):
            total = jnp.zeros((BAND, W), F32)
            for m in range(BLOCKS):
                block = jnp.where(up, tr[c, :BAND, m * W:(m + 1) * W], tr[c, BAND:, m * W:(m + 1) * W])
                total = jnp.where(column_mask(p, m), block, total)
            wsend[0, p, c] = total.astype(BF16)

    pl.semaphore_wait(barrier, 2 + len(peers))

    def halo_copy(i):
        return pltpu.make_async_remote_copy(
            src_ref=halo_send.at[i], dst_ref=halo.at[1 - i],
            send_sem=hs.at[i], recv_sem=hr.at[1 - i],
            device_id=(above if i == 0 else below, me), device_id_type=MESH,
        )

    def window_copy(h, p):
        return pltpu.make_async_remote_copy(
            src_ref=wsend.at[h, p], dst_ref=wrecv.at[h, me],
            send_sem=ws.at[h, p], recv_sem=wr.at[h, me],
            device_id=(t, p), device_id_type=MESH,
        )

    def window_arrival(h, k):
        return pltpu.make_async_remote_copy(
            src_ref=wsend.at[h, k], dst_ref=wrecv.at[h, k],
            send_sem=ws.at[h, k], recv_sem=wr.at[h, k],
            device_id=(t, k), device_id_type=MESH,
        )

    halo_copies = [halo_copy(i) for i in range(2)]
    for c in halo_copies:
        c.start()
    for p in reversed(peers):
        window_copy(0, p).start()
    wrecv[0, me] = wsend[0, me]

    fetches[2].wait()
    gcos[...] = jnp.cos(phase[...])
    gsin[...] = jnp.sin(phase[...])
    my_off = offset_of(me)
    my_col = pos_ref[me, 1]
    rows = lax.broadcasted_iota(jnp.int32, (W, W), 0)
    extended = my_off + ((rows - my_off + W) & (W - 1))
    inside = (extended >= -ext_ref[0, 0]) & (extended < STRIP + ext_ref[0, 1])
    fetches[1].wait()
    for c in range(2):
        turned = pltpu.roll(probe[c], (my_off + W) & (W - 1), 0)
        turned = pltpu.roll(turned, my_col & (W - 1), 1)
        waves[0, c] = jnp.where(inside, turned, 0.0)

    for c in halo_copies:
        c.wait()
    for p in range(DEPTH):
        up = upward(p)
        from_halo = jnp.where(up, half_rows - (BAND + offs[p]), offs[p] - 1 - half_rows) >= 0
        for c in range(2):
            total = jnp.zeros((BAND, W), F32)
            for m in range(BLOCKS):
                lanes = slice(m * W, (m + 1) * W)
                outer = jnp.where(up, halo[0, c, :, lanes].astype(F32), halo[1, c, :, lanes].astype(F32))
                inner = jnp.where(up, tr[c, BAND:, lanes], tr[c, :BAND, lanes])
                block = jnp.where(from_halo, outer, inner)
                total = jnp.where(column_mask(p, m), block, total)
            wsend[1, p, c] = total.astype(BF16)
    for p in reversed(peers):
        window_copy(1, p).start()
    wrecv[1, me] = wsend[1, me]

    for i in (3, 4, 5):
        fetches[i].wait()

    up_me = (half_rows * 0 + my_off) <= 0

    def layer(k):
        both = []
        for c in range(2):
            certain = wrecv[0, k, c].astype(F32)
            mixed = wrecv[1, k, c].astype(F32)
            both.append(jnp.concatenate(
                [jnp.where(up_me, certain, mixed), jnp.where(up_me, mixed, certain)], axis=0))
        return both

    def split(x, exact):
        high = x.astype(BF16)
        if not exact:
            return high, None
        return high, (x - high.astype(F32)).astype(BF16)

    def transform(re, im, inverse, exact):
        d = 1 if inverse else 0
        high, low = split(jnp.concatenate([re, im], axis=1), exact)
        parts = [high, high] + ([low] if exact else [])
        depth = len(parts) * 2 * W
        u = jnp.dot(jnp.concatenate(parts, axis=1), right[d, :depth, :], preferred_element_type=F32)
        high, low = split(jnp.concatenate([u[:, :W], u[:, W:]], axis=0), exact)
        parts = [high, high] + ([low] if exact else [])
        v = jnp.dot(left[d, :, :depth], jnp.concatenate(parts, axis=0), preferred_element_type=F32)
        return v[:W], v[W:]

    def propagate(re, im, conjugate, exact):
        re, im = transform(re, im, False, exact)
        co, si = gcos[...], gsin[...]
        if conjugate:
            re, im = re * co + im * si, im * co - re * si
        else:
            re, im = re * co - im * si, im * co + re * si
        return transform(re, im, True, exact)

    re = im = None
    for k in range(DEPTH):
        for h in range(2):
            @pl.when(me != k)
            def _():
                window_arrival(h, k).wait_recv()
        o_re, o_im = layer(k)
        if k == 0:
            re, im = waves[0, 0], waves[0, 1]
        else:
            waves[k, 0] = re
            waves[k, 1] = im
        re, im = re * o_re - im * o_im, re * o_im + im * o_re
        if k + 1 < DEPTH:
            re, im = propagate(re, im, False, True)
    re, im = transform(re, im, False, True)
    misfit = re * re + im * im - meas[...]
    re, im = transform(misfit * re, misfit * im, True, False)

    up_full = (rows * 0 + my_off) <= 0

    def gradient_copy(k, h):
        return pltpu.make_async_remote_copy(
            src_ref=gsend.at[h, k], dst_ref=grecv.at[h, me],
            send_sem=gs.at[h, k], recv_sem=gr.at[h, me],
            device_id=(t, k), device_id_type=MESH,
        )

    def gradient_arrival(p, h):
        return pltpu.make_async_remote_copy(
            src_ref=gsend.at[h, p], dst_ref=grecv.at[h, p],
            send_sem=gs.at[h, p], recv_sem=gr.at[h, p],
            device_id=(t, p), device_id_type=MESH,
        )

    for k in reversed(range(DEPTH)):
        if k + 1 < DEPTH:
            re, im = propagate(re, im, True, False)
        w_re, w_im = waves[k, 0], waves[k, 1]
        terms = (w_re * re + w_im * im, w_re * im - w_im * re)
        for c in range(2):
            lower, upper = terms[c][:BAND], terms[c][BAND:]
            gsend[1, k, c] = jnp.where(up_me, upper, lower).astype(BF16)
            gsend[0, k, c] = jnp.where(up_me, lower, upper).astype(BF16)

        @pl.when(me != k)
        def _():
            gradient_copy(k, 1).start()
            gradient_copy(k, 0).start()

        @pl.when(me == k)
        def _():
            grecv[1, me] = gsend[1, k]
            grecv[0, me] = gsend[0, k]

        if k > 0:
            o_re, o_im = layer(k)
            re, im = o_re * re + o_im * im, o_re * im - o_im * re

    for p in peers:
        gradient_arrival(p, 1).wait_recv()
    for c in range(2):
        for m in range(BLOCKS):
            lanes = slice(m * W, (m + 1) * W)
            top = bottom = jnp.zeros((BAND, W), F32)
            for p in range(DEPTH):
                up = upward(p)
                from_halo = jnp.where(up, half_rows - (BAND + offs[p]), offs[p] - 1 - half_rows) >= 0
                piece = jnp.where(from_halo & column_mask(p, m), grecv[1, p, c].astype(F32), 0.0)
                top = top + jnp.where(up, piece, 0.0)
                bottom = bottom + jnp.where(up, 0.0, piece)
            band_send[0, c, :, lanes] = top.astype(BF16)
            band_send[1, c, :, lanes] = bottom.astype(BF16)

    def band_copy(i):
        return pltpu.make_async_remote_copy(
            src_ref=band_send.at[i], dst_ref=band_recv.at[1 - i],
            send_sem=bs.at[i], recv_sem=br.at[1 - i],
            device_id=(above if i == 0 else below, me), device_id_type=MESH,
        )

    band_copies = [band_copy(i) for i in range(2)]
    for c in band_copies:
        c.start()
    for p in peers:
        gradient_arrival(p, 0).wait_recv()
    for c in range(2):
        for m in range(BLOCKS):
            lanes = slice(m * W, (m + 1) * W)
            top = bottom = jnp.zeros((BAND, W), F32)
            for p in range(DEPTH):
                up = upward(p)
                from_halo = jnp.where(up, half_rows - (BAND + offs[p]), offs[p] - 1 - half_rows) >= 0
                mask = column_mask(p, m)
                certain = jnp.where(mask, grecv[0, p, c].astype(F32), 0.0)
                mixed = jnp.where(mask & ~from_halo, grecv[1, p, c].astype(F32), 0.0)
                top = top + jnp.where(up, certain, mixed)
                bottom = bottom + jnp.where(up, mixed, certain)
            out_ref[c, 0, :BAND, lanes] = top
            out_ref[c, 0, BAND:, lanes] = bottom
    for i, c in enumerate(band_copies):
        c.wait()
    for i in range(2):
        edge = slice(i * BAND, (i + 1) * BAND)
        out_ref[:, 0, edge, :] = out_ref[:, 0, edge, :] + band_recv[i].astype(F32)
    for h in range(2):
        for p in peers:
            window_copy(h, p).wait_send()
            gradient_copy(p, h).wait_send()


def shards(tile_count, transmission, probe_wave, fresnel_phase, measured, positions, extents):
    right, left = dft_matrices()
    any_spec = pl.BlockSpec(memory_space=pl.ANY)
    smem = pl.BlockSpec(memory_space=pltpu.SMEM)
    dma = pltpu.SemaphoreType.DMA

    def body(*refs):
        kernel(tile_count, *refs)

    return pl.pallas_call(
        body,
        out_shape=jax.ShapeDtypeStruct(transmission.shape, F32),
        in_specs=[smem, smem] + [any_spec] * 6,
        out_specs=pl.BlockSpec(memory_space=pltpu.VMEM),
        scratch_shapes=[
            pltpu.VMEM((2, STRIP, OW), F32),
            pltpu.VMEM((2, W, W), F32),
            pltpu.VMEM((W, W), F32),
            pltpu.VMEM((W, W), F32),
            pltpu.VMEM(right.shape, BF16),
            pltpu.VMEM(left.shape, BF16),
            pltpu.VMEM((W, W), F32),
            pltpu.VMEM((W, W), F32),
            pltpu.VMEM((DEPTH, 2, W, W), F32),
            pltpu.VMEM((2, 2, BAND, OW), BF16),
            pltpu.VMEM((2, 2, BAND, OW), BF16),
            pltpu.VMEM((2, DEPTH, 2, BAND, W), BF16),
            pltpu.VMEM((2, DEPTH, 2, BAND, W), BF16),
            pltpu.VMEM((2, DEPTH, 2, BAND, W), BF16),
            pltpu.VMEM((2, DEPTH, 2, BAND, W), BF16),
            pltpu.VMEM((2, 2, BAND, OW), BF16),
            pltpu.VMEM((2, 2, BAND, OW), BF16),
            dma((6,)), dma((2,)), dma((2,)), dma((2, DEPTH)), dma((2, DEPTH)),
            dma((2, DEPTH)), dma((2, DEPTH)), dma((2,)), dma((2,)),
        ],
        compiler_params=pltpu.CompilerParams(collective_id=0, has_side_effects=True),
    )(positions, extents, transmission, probe_wave, fresnel_phase, measured,
      jnp.asarray(right), jnp.asarray(left))


def solution(mesh):
    tile_count = mesh.shape["tile"]
    placed = (
        P(None, "depth", "tile", None),
        P(),
        P(),
        P("tile", None, None),
        P("tile", None),
        P("tile", None),
    )

    def body(*args):
        return shards(tile_count, *args)

    return jax.shard_map(
        body,
        mesh=mesh,
        in_specs=placed,
        out_specs=P(None, "depth", "tile", None),
        check_vma=False,
    )
```

```python
import math

import jax
import jax.numpy as jnp
import numpy as np
from jax import lax
from jax.experimental import pallas as pl
from jax.experimental.pallas import tpu as pltpu
from jax.sharding import PartitionSpec as P

BAND = 64
W = 128
STRIP = 128
OW = 512
BLOCKS = OW // W
DEPTH = 4
RUN = 16
F32 = jnp.float32
BF16 = jnp.bfloat16
MESH = pl.DeviceIdType.MESH


def dft_matrices():
    index = np.arange(W)
    angles = (index[:, None] * index[None, :] % W) * (2.0 * math.pi / W)
    cosine = np.cos(angles) / math.sqrt(W)
    sine = np.sin(angles) / math.sqrt(W)
    a = np.block([[cosine, sine], [-sine, cosine]])
    b = a.T
    parts = []
    for m in (a, b):
        high = m.astype(BF16)
        low = (m - high.astype(np.float64)).astype(BF16)
        parts.append((high, low))
    right = np.stack([np.concatenate([h, l, h], axis=0) for h, l in (parts[1], parts[0])])
    left = np.stack([np.concatenate([h, l, h], axis=1) for h, l in (parts[0], parts[1])])
    return right, left


def kernel(
    tile_count,
    pos_ref, ext_ref, tr_hbm, probe_hbm, phase_hbm, meas_hbm, right_hbm, left_hbm,
    out_ref,
    tr, probe, phase, meas, right, left, gcos, gsin, waves,
    halo_send, halo, wsend, wrecv, gsend, grecv, band_send, band_recv, far_send, far_recv, col_send, col_recv,
    local_sem, hs, hr, ws, wr, gs, gr, bs, br, fs, fr, cs, cr,
):
    t = lax.axis_index("tile")
    me = lax.axis_index("depth")
    above = lax.rem(t + tile_count - 1, tile_count)
    below = lax.rem(t + 1, tile_count)
    peers = [lax.rem(me + j, DEPTH) for j in range(1, DEPTH)]

    sides = (above, below)

    def at_end(tile):
        place = lax.rem(tile, RUN)
        return (place == 0) | (place == RUN - 1)

    end_me = at_end(t)
    end_side = (at_end(above), at_end(below))

    barrier = pltpu.get_barrier_semaphore()
    for side in sides:
        pl.semaphore_signal(barrier, inc=1, device_id=(side, me), device_id_type=MESH)
    expected = 2 + len(peers)
    for i in range(2):
        wide = end_me | end_side[i]
        expected = expected + jnp.where(wide, len(peers), 0)

        @pl.when(wide)
        def _():
            for p in peers:
                pl.semaphore_signal(barrier, inc=1, device_id=(sides[i], p), device_id_type=MESH)

    for p in peers:
        pl.semaphore_signal(barrier, inc=1, device_id=(t, p), device_id_type=MESH)

    fetches = [
        pltpu.make_async_copy(tr_hbm.at[:, 0], tr, local_sem.at[0]),
        pltpu.make_async_copy(probe_hbm, probe, local_sem.at[1]),
        pltpu.make_async_copy(phase_hbm, phase, local_sem.at[2]),
        pltpu.make_async_copy(meas_hbm.at[me], meas, local_sem.at[3]),
        pltpu.make_async_copy(right_hbm, right, local_sem.at[4]),
        pltpu.make_async_copy(left_hbm, left, local_sem.at[5]),
    ]
    for f in fetches:
        f.start()

    def offset_of(p):
        rows = STRIP * tile_count
        return lax.rem(pos_ref[0, p] - t * STRIP + (rows + BAND), rows) - BAND

    offs = [offset_of(p) for p in range(DEPTH)]
    cols = [pos_ref[1, p] for p in range(DEPTH)]

    half_rows = lax.broadcasted_iota(jnp.int32, (BAND, W), 0)
    half_lanes = lax.broadcasted_iota(jnp.int32, (BAND, W), 1)

    def column_mask(p, m):
        position = half_lanes + m * W
        return (position >= cols[p]) & (position < cols[p] + W)

    def upward(p):
        return (half_rows * 0 + offs[p]) <= 0

    fetches[0].wait()
    for i in range(2):
        halo_send[i] = tr[:, i * BAND:(i + 1) * BAND, :].astype(BF16)

    for p in range(DEPTH):
        up = upward(p)
        for c in range(2):
            total = jnp.zeros((BAND, W), F32)
            for m in range(BLOCKS):
                block = jnp.where(up, tr[c, :BAND, m * W:(m + 1) * W], tr[c, BAND:, m * W:(m + 1) * W])
                total = jnp.where(column_mask(p, m), block, total)
            wsend[0, p, c] = total.astype(BF16)

    which = lax.broadcasted_iota(jnp.int32, (8, W), 0)
    columns = which * 0
    for p in range(DEPTH):
        columns = jnp.where(which == p, cols[p], columns)
    col_send[...] = columns.astype(F32)

    pl.semaphore_wait(barrier, expected)

    def halo_copy(i):
        return pltpu.make_async_remote_copy(
            src_ref=halo_send.at[i], dst_ref=halo.at[1 - i],
            send_sem=hs.at[i], recv_sem=hr.at[1 - i],
            device_id=(above if i == 0 else below, me), device_id_type=MESH,
        )

    def window_copy(h, p):
        return pltpu.make_async_remote_copy(
            src_ref=wsend.at[h, p], dst_ref=wrecv.at[h, me],
            send_sem=ws.at[h, p], recv_sem=wr.at[h, me],
            device_id=(t, p), device_id_type=MESH,
        )

    def window_arrival(h, k):
        return pltpu.make_async_remote_copy(
            src_ref=wsend.at[h, k], dst_ref=wrecv.at[h, k],
            send_sem=ws.at[h, k], recv_sem=wr.at[h, k],
            device_id=(t, k), device_id_type=MESH,
        )

    halo_copies = [halo_copy(i) for i in range(2)]
    for c in halo_copies:
        c.start()
    for p in reversed(peers):
        window_copy(0, p).start()
    wrecv[0, me] = wsend[0, me]

    def column_copy(i):
        return pltpu.make_async_remote_copy(
            src_ref=col_send, dst_ref=col_recv.at[1 - i],
            send_sem=cs.at[i], recv_sem=cr.at[1 - i],
            device_id=(sides[i], me), device_id_type=MESH,
        )

    @pl.when(end_me)
    def _():
        for i in range(2):
            column_copy(i).start()

    fetches[2].wait()
    gcos[...] = jnp.cos(phase[...])
    gsin[...] = jnp.sin(phase[...])
    my_off = offset_of(me)
    my_col = pos_ref[1, me]
    rows = lax.broadcasted_iota(jnp.int32, (W, W), 0)
    extended = my_off + ((rows - my_off + W) & (W - 1))
    inside = (extended >= -ext_ref[0, 0]) & (extended < STRIP + ext_ref[0, 1])
    fetches[1].wait()
    for c in range(2):
        turned = pltpu.roll(probe[c], (my_off + W) & (W - 1), 0)
        turned = pltpu.roll(turned, my_col & (W - 1), 1)
        waves[0, c] = jnp.where(inside, turned, 0.0)

    for c in halo_copies:
        c.wait()
    for p in range(DEPTH):
        up = upward(p)
        from_halo = jnp.where(up, half_rows - (BAND + offs[p]), offs[p] - 1 - half_rows) >= 0
        for c in range(2):
            total = jnp.zeros((BAND, W), F32)
            for m in range(BLOCKS):
                lanes = slice(m * W, (m + 1) * W)
                outer = jnp.where(up, halo[0, c, :, lanes].astype(F32), halo[1, c, :, lanes].astype(F32))
                inner = jnp.where(up, tr[c, BAND:, lanes], tr[c, :BAND, lanes])
                block = jnp.where(from_halo, outer, inner)
                total = jnp.where(column_mask(p, m), block, total)
            wsend[1, p, c] = total.astype(BF16)
    for p in reversed(peers):
        window_copy(1, p).start()
    wrecv[1, me] = wsend[1, me]

    for i in (3, 4, 5):
        fetches[i].wait()

    up_me = (half_rows * 0 + my_off) <= 0

    def layer(k):
        both = []
        for c in range(2):
            certain = wrecv[0, k, c].astype(F32)
            mixed = wrecv[1, k, c].astype(F32)
            both.append(jnp.concatenate(
                [jnp.where(up_me, certain, mixed), jnp.where(up_me, mixed, certain)], axis=0))
        return both

    def split(x, exact):
        high = x.astype(BF16)
        if not exact:
            return high, None
        return high, (x - high.astype(F32)).astype(BF16)

    def transform(re, im, inverse, exact):
        d = 1 if inverse else 0
        high, low = split(jnp.concatenate([re, im], axis=1), exact)
        parts = [high, high] + ([low] if exact else [])
        depth = len(parts) * 2 * W
        u = jnp.dot(jnp.concatenate(parts, axis=1), right[d, :depth, :], preferred_element_type=F32)
        high, low = split(jnp.concatenate([u[:, :W], u[:, W:]], axis=0), exact)
        parts = [high, high] + ([low] if exact else [])
        v = jnp.dot(left[d, :, :depth], jnp.concatenate(parts, axis=0), preferred_element_type=F32)
        return v[:W], v[W:]

    def propagate(re, im, conjugate, exact):
        re, im = transform(re, im, False, exact)
        co, si = gcos[...], gsin[...]
        if conjugate:
            re, im = re * co + im * si, im * co - re * si
        else:
            re, im = re * co - im * si, im * co + re * si
        return transform(re, im, True, exact)

    re = im = None
    for k in range(DEPTH):
        for h in range(2):
            @pl.when(me != k)
            def _():
                window_arrival(h, k).wait_recv()
        o_re, o_im = layer(k)
        if k == 0:
            re, im = waves[0, 0], waves[0, 1]
        else:
            waves[k, 0] = re
            waves[k, 1] = im
        re, im = re * o_re - im * o_im, re * o_im + im * o_re
        if k + 1 < DEPTH:
            re, im = propagate(re, im, False, True)
    re, im = transform(re, im, False, True)
    misfit = re * re + im * im - meas[...]
    re, im = transform(misfit * re, misfit * im, True, False)

    from_halo_me = jnp.where(up_me, half_rows - (BAND + my_off), my_off - 1 - half_rows) >= 0

    def gradient_copy(k, h):
        return pltpu.make_async_remote_copy(
            src_ref=gsend.at[h, k], dst_ref=grecv.at[h, me],
            send_sem=gs.at[h, k], recv_sem=gr.at[h, me],
            device_id=(t, k), device_id_type=MESH,
        )

    def far_copy(i, k):
        return pltpu.make_async_remote_copy(
            src_ref=far_send.at[i, k], dst_ref=far_recv.at[1 - i, me],
            send_sem=fs.at[i, k], recv_sem=fr.at[1 - i, me],
            device_id=(sides[i], k), device_id_type=MESH,
        )

    def far_arrival(i, p):
        return pltpu.make_async_remote_copy(
            src_ref=far_send.at[i, p], dst_ref=far_recv.at[i, p],
            send_sem=fs.at[i, p], recv_sem=fr.at[i, p],
            device_id=(sides[i], p), device_id_type=MESH,
        )

    def gradient_arrival(p, h):
        return pltpu.make_async_remote_copy(
            src_ref=gsend.at[h, p], dst_ref=grecv.at[h, p],
            send_sem=gs.at[h, p], recv_sem=gr.at[h, p],
            device_id=(t, p), device_id_type=MESH,
        )

    for k in reversed(range(DEPTH)):
        if k + 1 < DEPTH:
            re, im = propagate(re, im, True, False)
        w_re, w_im = waves[k, 0], waves[k, 1]
        terms = (w_re * re + w_im * im, w_re * im - w_im * re)

        @pl.when(end_me)
        def _():
            for c in range(2):
                mixed = jnp.where(up_me, terms[c][BAND:], terms[c][:BAND])
                mixed = jnp.where(from_halo_me, mixed, 0.0)
                far_send[0, k, c] = jnp.where(up_me, mixed, 0.0).astype(BF16)
                far_send[1, k, c] = jnp.where(up_me, 0.0, mixed).astype(BF16)
            for i in range(2):
                far_copy(i, k).start()

        for c in range(2):
            lower, upper = terms[c][:BAND], terms[c][BAND:]
            gsend[1, k, c] = jnp.where(up_me, upper, lower).astype(BF16)
            gsend[0, k, c] = jnp.where(up_me, lower, upper).astype(BF16)

        @pl.when(me != k)
        def _():
            gradient_copy(k, 1).start()
            gradient_copy(k, 0).start()

        @pl.when(me == k)
        def _():
            grecv[1, me] = gsend[1, k]
            grecv[0, me] = gsend[0, k]

        if k > 0:
            o_re, o_im = layer(k)
            re, im = o_re * re + o_im * im, o_re * im - o_im * re

    for p in peers:
        gradient_arrival(p, 1).wait_recv()
    def band_copy(i):
        return pltpu.make_async_remote_copy(
            src_ref=band_send.at[i], dst_ref=band_recv.at[1 - i],
            send_sem=bs.at[i], recv_sem=br.at[1 - i],
            device_id=(above if i == 0 else below, me), device_id_type=MESH,
        )

    @pl.when(~end_me)
    def _():
        for c in range(2):
            for m in range(BLOCKS):
                lanes = slice(m * W, (m + 1) * W)
                top = bottom = jnp.zeros((BAND, W), F32)
                for p in range(DEPTH):
                    up = upward(p)
                    from_halo = jnp.where(up, half_rows - (BAND + offs[p]), offs[p] - 1 - half_rows) >= 0
                    piece = jnp.where(from_halo & column_mask(p, m), grecv[1, p, c].astype(F32), 0.0)
                    top = top + jnp.where(up, piece, 0.0)
                    bottom = bottom + jnp.where(up, 0.0, piece)
                band_send[0, c, :, lanes] = top.astype(BF16)
                band_send[1, c, :, lanes] = bottom.astype(BF16)
        for i in range(2):
            band_copy(i).start()

    for p in peers:
        gradient_arrival(p, 0).wait_recv()
    for c in range(2):
        for m in range(BLOCKS):
            lanes = slice(m * W, (m + 1) * W)
            top = bottom = jnp.zeros((BAND, W), F32)
            for p in range(DEPTH):
                up = upward(p)
                from_halo = jnp.where(up, half_rows - (BAND + offs[p]), offs[p] - 1 - half_rows) >= 0
                mask = column_mask(p, m)
                certain = jnp.where(mask, grecv[0, p, c].astype(F32), 0.0)
                mixed = jnp.where(mask & ~from_halo, grecv[1, p, c].astype(F32), 0.0)
                top = top + jnp.where(up, certain, mixed)
                bottom = bottom + jnp.where(up, mixed, certain)
            out_ref[c, 0, :BAND, lanes] = top
            out_ref[c, 0, BAND:, lanes] = bottom
    lanes_f = half_lanes.astype(F32)
    for i in range(2):
        edge = slice(i * BAND, (i + 1) * BAND)

        @pl.when(~end_side[i])
        def _():
            band_copy(1 - i).wait_recv()
            out_ref[:, 0, edge, :] = out_ref[:, 0, edge, :] + band_recv[i].astype(F32)

        @pl.when(end_side[i])
        def _():
            column_copy(1 - i).wait_recv()
            for p in range(DEPTH):
                far_arrival(i, p).wait_recv()
            for m in range(BLOCKS):
                lanes = slice(m * W, (m + 1) * W)
                totals = [out_ref[c, 0, edge, lanes] for c in range(2)]
                for p in range(DEPTH):
                    start = col_recv[i, p:p + 1, :] - float(m * W)
                    mask = (lanes_f >= start) & (lanes_f < start + float(W))
                    for c in range(2):
                        totals[c] = totals[c] + jnp.where(mask, far_recv[i, p, c].astype(F32), 0.0)
                for c in range(2):
                    out_ref[c, 0, edge, lanes] = totals[c]

    @pl.when(~end_me)
    def _():
        for i in range(2):
            band_copy(i).wait_send()

    @pl.when(end_me)
    def _():
        for i in range(2):
            column_copy(i).wait_send()
            for k in range(DEPTH):
                far_copy(i, k).wait_send()

    for h in range(2):
        for p in peers:
            window_copy(h, p).wait_send()
            gradient_copy(p, h).wait_send()


def shards(tile_count, transmission, probe_wave, fresnel_phase, measured, positions, extents):
    right, left = dft_matrices()
    any_spec = pl.BlockSpec(memory_space=pl.ANY)
    smem = pl.BlockSpec(memory_space=pltpu.SMEM)
    dma = pltpu.SemaphoreType.DMA

    def body(*refs):
        kernel(tile_count, *refs)

    return pl.pallas_call(
        body,
        out_shape=pltpu.VMEM(transmission.shape, F32),
        in_specs=[smem, smem] + [any_spec] * 6,
        out_specs=pl.BlockSpec(memory_space=pltpu.VMEM),
        scratch_shapes=[
            pltpu.VMEM((2, STRIP, OW), F32),
            pltpu.VMEM((2, W, W), F32),
            pltpu.VMEM((W, W), F32),
            pltpu.VMEM((W, W), F32),
            pltpu.VMEM(right.shape, BF16),
            pltpu.VMEM(left.shape, BF16),
            pltpu.VMEM((W, W), F32),
            pltpu.VMEM((W, W), F32),
            pltpu.VMEM((DEPTH, 2, W, W), F32),
            pltpu.VMEM((2, 2, BAND, OW), BF16),
            pltpu.VMEM((2, 2, BAND, OW), BF16),
            pltpu.VMEM((2, DEPTH, 2, BAND, W), BF16),
            pltpu.VMEM((2, DEPTH, 2, BAND, W), BF16),
            pltpu.VMEM((2, DEPTH, 2, BAND, W), BF16),
            pltpu.VMEM((2, DEPTH, 2, BAND, W), BF16),
            pltpu.VMEM((2, 2, BAND, OW), BF16),
            pltpu.VMEM((2, 2, BAND, OW), BF16),
            pltpu.VMEM((2, DEPTH, 2, BAND, W), BF16),
            pltpu.VMEM((2, DEPTH, 2, BAND, W), BF16),
            pltpu.VMEM((8, W), F32),
            pltpu.VMEM((2, 8, W), F32),
            dma((6,)), dma((2,)), dma((2,)), dma((2, DEPTH)), dma((2, DEPTH)),
            dma((2, DEPTH)), dma((2, DEPTH)), dma((2,)), dma((2,)),
            dma((2, DEPTH)), dma((2, DEPTH)), dma((2,)), dma((2,)),
        ],
        compiler_params=pltpu.CompilerParams(collective_id=0, has_side_effects=True, vmem_limit_bytes=66506752),
    )(positions.T, extents, transmission, probe_wave, fresnel_phase, measured,
      jnp.asarray(right), jnp.asarray(left))


def solution(mesh):
    tile_count = mesh.shape["tile"]
    placed = (
        P(None, "depth", "tile", None),
        P(),
        P(),
        P("tile", None, None),
        P("tile", None),
        P("tile", None),
    )

    def body(*args):
        return shards(tile_count, *args)

    return jax.shard_map(
        body,
        mesh=mesh,
        in_specs=placed,
        out_specs=P(None, "depth", "tile", None),
        check_vma=False,
    )
```

```python
import math

import jax
import jax.numpy as jnp
import numpy as np
from jax import lax
from jax.experimental import pallas as pl
from jax.experimental.pallas import tpu as pltpu
from jax.sharding import PartitionSpec as P

BAND = 64
W = 128
STRIP = 128
OW = 512
BLOCKS = OW // W
DEPTH = 4
RUN = 16
PARTS = 2
FORWARD = (3, 3)
TURN = (2, 2)
BACKWARD = (2, 2)
PART = BAND // PARTS
F32 = jnp.float32
BF16 = jnp.bfloat16
MESH = pl.DeviceIdType.MESH


def dft_matrices():
    index = np.arange(W)
    angles = (index[:, None] * index[None, :] % W) * (2.0 * math.pi / W)
    cosine = np.cos(angles) / math.sqrt(W)
    sine = np.sin(angles) / math.sqrt(W)
    a = np.block([[cosine, sine], [-sine, cosine]])
    b = a.T
    parts = []
    for m in (a, b):
        high = m.astype(BF16)
        low = (m - high.astype(np.float64)).astype(BF16)
        parts.append((high, low))
    right = np.stack([np.concatenate([h, l, h], axis=0) for h, l in (parts[1], parts[0])])
    left = np.stack([np.concatenate([h, l, h], axis=1) for h, l in (parts[0], parts[1])])
    return right, left


def kernel(
    tile_count,
    pos_hbm, ext_hbm, tr_hbm, probe_hbm, phase_hbm, meas_hbm, right_hbm, left_hbm,
    out_ref,
    tr, probe, phase, meas, right, left, gcos, gsin, waves,
    halo_send, halo, wsend, wrecv, gsend, grecv, band_send, band_recv, far_send, far_recv, col_send, col_recv, pos_ref, ext_ref,
    local_sem, hs, hr, ws, wr, gs, gr, bs, br, fs, fr, cs, cr,
):
    t = lax.axis_index("tile")
    me = lax.axis_index("depth")
    above = lax.rem(t + tile_count - 1, tile_count)
    below = lax.rem(t + 1, tile_count)
    peers = [lax.rem(me + j, DEPTH) for j in range(1, DEPTH)]

    sides = (above, below)

    def straight(tile):
        place = lax.rem(tile, RUN)
        return (place == 0) | (place == RUN - 1)

    out_straight = [straight(t)] * 2
    in_straight = [straight(side) for side in sides]
    even = lax.rem(lax.div(t, RUN), 2) == 0
    urgent = jnp.where((lax.rem(t, RUN) == 0) == even, 1, 0)

    barrier = pltpu.get_barrier_semaphore()
    for side in sides:
        pl.semaphore_signal(barrier, inc=1, device_id=(side, me), device_id_type=MESH)
    expected = 2 + len(peers)
    for i in range(2):
        for p in peers:
            wide = out_straight[i] | in_straight[i]
            expected = expected + jnp.where(wide, 1, 0)

            @pl.when(wide)
            def _():
                pl.semaphore_signal(barrier, inc=1, device_id=(sides[i], p), device_id_type=MESH)

    for p in peers:
        pl.semaphore_signal(barrier, inc=1, device_id=(t, p), device_id_type=MESH)

    fetches = [
        pltpu.make_async_copy(tr_hbm.at[:, 0], tr, local_sem.at[0]),
        pltpu.make_async_copy(probe_hbm, probe, local_sem.at[1]),
        pltpu.make_async_copy(phase_hbm, phase, local_sem.at[2]),
        pltpu.make_async_copy(meas_hbm.at[me], meas, local_sem.at[3]),
        pltpu.make_async_copy(right_hbm, right, local_sem.at[4]),
        pltpu.make_async_copy(left_hbm, left, local_sem.at[5]),
        pltpu.make_async_copy(pos_hbm, pos_ref, local_sem.at[6]),
        pltpu.make_async_copy(ext_hbm, ext_ref, local_sem.at[7]),
    ]
    for i in (6, 7, 0):
        fetches[i].start()
    for f in fetches[6:]:
        f.wait()

    def offset_of(p):
        rows = STRIP * tile_count
        return lax.rem(pos_ref[0, p] - t * STRIP + (rows + BAND), rows) - BAND

    offs = [offset_of(p) for p in range(DEPTH)]
    cols = [pos_ref[1, p] for p in range(DEPTH)]
    order = list(reversed(peers)) + [me]

    half_rows = lax.broadcasted_iota(jnp.int32, (BAND, W), 0)
    half_lanes = lax.broadcasted_iota(jnp.int32, (BAND, W), 1)

    def column_mask(p, m):
        position = half_lanes + m * W
        return (position >= cols[p]) & (position < cols[p] + W)

    def upward(p):
        return (half_rows * 0 + offs[p]) <= 0

    fetches[0].wait()
    for i in range(2):
        halo_send[i] = tr[:, i * BAND:(i + 1) * BAND, :].astype(BF16)

    which = lax.broadcasted_iota(jnp.int32, (8, W), 0)
    columns = which * 0
    for p in range(DEPTH):
        columns = jnp.where(which == p, cols[p], columns)
    col_send[...] = columns.astype(F32)

    pl.semaphore_wait(barrier, expected)

    def part_rows(q):
        return slice(q * PART, (q + 1) * PART)

    def halo_copy(i, q):
        return pltpu.make_async_remote_copy(
            src_ref=halo_send.at[i, :, part_rows(q)], dst_ref=halo.at[1 - i, :, part_rows(q)],
            send_sem=hs.at[i, q], recv_sem=hr.at[1 - i, q],
            device_id=(sides[i], me), device_id_type=MESH,
        )

    def window_part(ref, h, k):
        return ref.at[0, k] if h == 0 else ref.at[1, k, :, part_rows(h - 1)]

    def window_copy(h, p):
        return pltpu.make_async_remote_copy(
            src_ref=window_part(wsend, h, p), dst_ref=window_part(wrecv, h, me),
            send_sem=ws.at[h, p], recv_sem=wr.at[h, me],
            device_id=(t, p), device_id_type=MESH,
        )

    def window_arrival(h, k):
        return pltpu.make_async_remote_copy(
            src_ref=window_part(wsend, h, k), dst_ref=window_part(wrecv, h, k),
            send_sem=ws.at[h, k], recv_sem=wr.at[h, k],
            device_id=(t, k), device_id_type=MESH,
        )

    for q in range(PARTS):
        for i in range(2):
            halo_copy(i, q).start()
    for i in range(1, 6):
        fetches[i].start()

    def cut_masks(p):
        start = pos_ref[1, p]
        shift = offset_of(p)
        up = (half_rows * 0 + shift) <= 0
        outside = jnp.where(up, half_rows - (BAND + shift), shift - 1 - half_rows) >= 0
        lanes = [(half_lanes + m * W >= start) & (half_lanes + m * W < start + W) for m in range(BLOCKS)]
        return up, outside, lanes

    for p in order:
        up, _, picks = cut_masks(p)
        for c in range(2):
            total = jnp.zeros((BAND, W), F32)
            for m in range(BLOCKS):
                lanes = slice(m * W, (m + 1) * W)
                total = jnp.where(picks[m], jnp.where(up, tr[c, :BAND, lanes], tr[c, BAND:, lanes]), total)
            if p is me:
                wrecv[0, me, c] = total.astype(BF16)
            else:
                wsend[0, p, c] = total.astype(BF16)
        if p is not me:
            window_copy(0, p).start()

    def column_copy(i):
        return pltpu.make_async_remote_copy(
            src_ref=col_send, dst_ref=col_recv.at[1 - i],
            send_sem=cs.at[i], recv_sem=cr.at[1 - i],
            device_id=(sides[i], me), device_id_type=MESH,
        )

    for i in range(2):
        @pl.when(out_straight[i])
        def _():
            column_copy(i).start()

    fetches[2].wait()
    gcos[...] = jnp.cos(phase[...])
    gsin[...] = jnp.sin(phase[...])
    my_off = offset_of(me)
    my_col = pos_ref[1, me]
    rows = lax.broadcasted_iota(jnp.int32, (W, W), 0)
    extended = my_off + ((rows - my_off + W) & (W - 1))
    inside = (extended >= -ext_ref[0, 0]) & (extended < STRIP + ext_ref[0, 1])
    fetches[1].wait()
    for c in range(2):
        turned = pltpu.roll(probe[c], (my_off + W) & (W - 1), 0)
        turned = pltpu.roll(turned, my_col & (W - 1), 1)
        waves[0, c] = jnp.where(inside, turned, 0.0)

    for q in range(PARTS):
        for i in range(2):
            halo_copy(i, q).wait_recv()
        for p in order:
            up, outside, picks = cut_masks(p)
            up, outside = up[part_rows(q)], outside[part_rows(q)]
            for c in range(2):
                total = jnp.zeros((PART, W), F32)
                for m in range(BLOCKS):
                    lanes = slice(m * W, (m + 1) * W)
                    outer = jnp.where(up, halo[0, c, part_rows(q), lanes].astype(F32), halo[1, c, part_rows(q), lanes].astype(F32))
                    inner = jnp.where(up, tr[c, BAND + q * PART:BAND + (q + 1) * PART, lanes], tr[c, part_rows(q), lanes])
                    total = jnp.where(picks[m][part_rows(q)], jnp.where(outside, outer, inner), total)
                if p is me:
                    wrecv[1, me, c, part_rows(q)] = total.astype(BF16)
                else:
                    wsend[1, p, c, part_rows(q)] = total.astype(BF16)
            if p is not me:
                window_copy(q + 1, p).start()

    for i in (3, 4, 5):
        fetches[i].wait()

    up_me = (half_rows * 0 + my_off) <= 0

    def layer(k):
        both = []
        for c in range(2):
            certain = wrecv[0, k, c].astype(F32)
            mixed = wrecv[1, k, c].astype(F32)
            both.append(jnp.concatenate(
                [jnp.where(up_me, certain, mixed), jnp.where(up_me, mixed, certain)], axis=0))
        return both

    def parts_of(x, products):
        high = x.astype(BF16)
        parts = [high] * min(products, 2)
        if products == 3:
            parts.append((x - high.astype(F32)).astype(BF16))
        return parts

    def transform(re, im, inverse, products):
        d = 1 if inverse else 0
        n_right, n_left = products
        x = jnp.concatenate([re, im], axis=1)
        u = jnp.dot(jnp.concatenate(parts_of(x, n_right), axis=1), right[d, :n_right * 2 * W, :],
                    preferred_element_type=F32)
        x = jnp.concatenate([u[:, :W], u[:, W:]], axis=0)
        v = jnp.dot(left[d, :, :n_left * 2 * W], jnp.concatenate(parts_of(x, n_left), axis=0),
                    preferred_element_type=F32)
        return v[:W], v[W:]

    def propagate(re, im, conjugate, products):
        re, im = transform(re, im, False, products)
        co, si = gcos[...], gsin[...]
        if conjugate:
            re, im = re * co + im * si, im * co - re * si
        else:
            re, im = re * co - im * si, im * co + re * si
        return transform(re, im, True, products)

    re = im = None
    for k in range(DEPTH):
        for h in range(1 + PARTS):
            @pl.when(me != k)
            def _():
                window_arrival(h, k).wait_recv()
        o_re, o_im = layer(k)
        if k == 0:
            re, im = waves[0, 0], waves[0, 1]
        else:
            waves[k, 0] = re
            waves[k, 1] = im
        re, im = re * o_re - im * o_im, re * o_im + im * o_re
        if k + 1 < DEPTH:
            re, im = propagate(re, im, False, FORWARD)
    re, im = transform(re, im, False, FORWARD)
    misfit = re * re + im * im - meas[...]
    re, im = transform(misfit * re, misfit * im, True, TURN)

    from_halo_me = jnp.where(up_me, half_rows - (BAND + my_off), my_off - 1 - half_rows) >= 0

    def gradient_copy(k, h):
        return pltpu.make_async_remote_copy(
            src_ref=gsend.at[h, k], dst_ref=grecv.at[h, me],
            send_sem=gs.at[h, k], recv_sem=gr.at[h, me],
            device_id=(t, k), device_id_type=MESH,
        )

    def far_copy(i, k):
        return pltpu.make_async_remote_copy(
            src_ref=far_send.at[i, k], dst_ref=far_recv.at[1 - i, me],
            send_sem=fs.at[i, k], recv_sem=fr.at[1 - i, me],
            device_id=(jnp.where(i == 0, above, below), k), device_id_type=MESH,
        )

    def far_arrival(i, p):
        return pltpu.make_async_remote_copy(
            src_ref=far_send.at[i, p], dst_ref=far_recv.at[i, p],
            send_sem=fs.at[i, p], recv_sem=fr.at[i, p],
            device_id=(sides[i], p), device_id_type=MESH,
        )

    def gradient_arrival(p, h):
        return pltpu.make_async_remote_copy(
            src_ref=gsend.at[h, p], dst_ref=grecv.at[h, p],
            send_sem=gs.at[h, p], recv_sem=gr.at[h, p],
            device_id=(t, p), device_id_type=MESH,
        )

    for k in reversed(range(DEPTH)):
        if k + 1 < DEPTH:
            re, im = propagate(re, im, True, BACKWARD)
        w_re, w_im = waves[k, 0], waves[k, 1]
        terms = (w_re * re + w_im * im, w_re * im - w_im * re)

        @pl.when(straight(t))
        def _():
            for c in range(2):
                mixed = jnp.where(up_me, terms[c][BAND:], terms[c][:BAND])
                mixed = jnp.where(from_halo_me, mixed, 0.0)
                far_send[0, k, c] = jnp.where(up_me, mixed, 0.0).astype(BF16)
                far_send[1, k, c] = jnp.where(up_me, 0.0, mixed).astype(BF16)
            far_copy(urgent, k).start()

        for c in range(2):
            lower, upper = terms[c][:BAND], terms[c][BAND:]
            gsend[1, k, c] = jnp.where(up_me, upper, lower).astype(BF16)
            gsend[0, k, c] = jnp.where(up_me, lower, upper).astype(BF16)

        @pl.when(me != k)
        def _():
            gradient_copy(k, 1).start()
            gradient_copy(k, 0).start()

        @pl.when(straight(t))
        def _():
            far_copy(1 - urgent, k).start()

        @pl.when(me == k)
        def _():
            grecv[1, me] = gsend[1, k]
            grecv[0, me] = gsend[0, k]

        if k > 0:
            o_re, o_im = layer(k)
            re, im = o_re * re + o_im * im, o_re * im - o_im * re

    for p in peers:
        gradient_arrival(p, 1).wait_recv()
    def band_copy(i):
        return pltpu.make_async_remote_copy(
            src_ref=band_send.at[i], dst_ref=band_recv.at[1 - i],
            send_sem=bs.at[i], recv_sem=br.at[1 - i],
            device_id=(above if i == 0 else below, me), device_id_type=MESH,
        )

    for c in range(2):
        for m in range(BLOCKS):
            lanes = slice(m * W, (m + 1) * W)
            top = bottom = jnp.zeros((BAND, W), F32)
            for p in range(DEPTH):
                up = upward(p)
                from_halo = jnp.where(up, half_rows - (BAND + offs[p]), offs[p] - 1 - half_rows) >= 0
                piece = jnp.where(from_halo & column_mask(p, m), grecv[1, p, c].astype(F32), 0.0)
                top = top + jnp.where(up, piece, 0.0)
                bottom = bottom + jnp.where(up, 0.0, piece)
            band_send[0, c, :, lanes] = top.astype(BF16)
            band_send[1, c, :, lanes] = bottom.astype(BF16)
    for i in range(2):
        @pl.when(~out_straight[i])
        def _():
            band_copy(i).start()

    for p in peers:
        gradient_arrival(p, 0).wait_recv()
    for c in range(2):
        for m in range(BLOCKS):
            lanes = slice(m * W, (m + 1) * W)
            top = bottom = jnp.zeros((BAND, W), F32)
            for p in range(DEPTH):
                up = upward(p)
                from_halo = jnp.where(up, half_rows - (BAND + offs[p]), offs[p] - 1 - half_rows) >= 0
                mask = column_mask(p, m)
                certain = jnp.where(mask, grecv[0, p, c].astype(F32), 0.0)
                mixed = jnp.where(mask & ~from_halo, grecv[1, p, c].astype(F32), 0.0)
                top = top + jnp.where(up, certain, mixed)
                bottom = bottom + jnp.where(up, mixed, certain)
            out_ref[c, 0, :BAND, lanes] = top
            out_ref[c, 0, BAND:, lanes] = bottom
    lanes_f = half_lanes.astype(F32)
    for i in range(2):
        edge = slice(i * BAND, (i + 1) * BAND)

        @pl.when(~in_straight[i])
        def _():
            band_copy(1 - i).wait_recv()
            out_ref[:, 0, edge, :] = out_ref[:, 0, edge, :] + band_recv[i].astype(F32)

        @pl.when(in_straight[i])
        def _():
            column_copy(1 - i).wait_recv()
            for p in range(DEPTH):
                far_arrival(i, p).wait_recv()
            for m in range(BLOCKS):
                lanes = slice(m * W, (m + 1) * W)
                totals = [out_ref[c, 0, edge, lanes] for c in range(2)]
                for p in range(DEPTH):
                    start = col_recv[i, p:p + 1, :] - float(m * W)
                    mask = (lanes_f >= start) & (lanes_f < start + float(W))
                    for c in range(2):
                        totals[c] = totals[c] + jnp.where(mask, far_recv[i, p, c].astype(F32), 0.0)
                for c in range(2):
                    out_ref[c, 0, edge, lanes] = totals[c]

    for i in range(2):
        @pl.when(~out_straight[i])
        def _():
            band_copy(i).wait_send()

        @pl.when(out_straight[i])
        def _():
            column_copy(i).wait_send()

        for k in range(DEPTH):
            @pl.when(out_straight[i])
            def _():
                far_copy(i, k).wait_send()

    for i in range(2):
        for q in range(PARTS):
            halo_copy(i, q).wait_send()
    for p in peers:
        for h in range(1 + PARTS):
            window_copy(h, p).wait_send()
        for h in range(2):
            gradient_copy(p, h).wait_send()


def shards(tile_count, transmission, probe_wave, fresnel_phase, measured, positions, extents):
    right, left = dft_matrices()
    any_spec = pl.BlockSpec(memory_space=pl.ANY)
    dma = pltpu.SemaphoreType.DMA

    def body(*refs):
        kernel(tile_count, *refs)

    return pl.pallas_call(
        body,
        out_shape=pltpu.VMEM(transmission.shape, F32),
        in_specs=[any_spec] * 8,
        out_specs=pl.BlockSpec(memory_space=pltpu.VMEM),
        scratch_shapes=[
            pltpu.VMEM((2, STRIP, OW), F32),
            pltpu.VMEM((2, W, W), F32),
            pltpu.VMEM((W, W), F32),
            pltpu.VMEM((W, W), F32),
            pltpu.VMEM(right.shape, BF16),
            pltpu.VMEM(left.shape, BF16),
            pltpu.VMEM((W, W), F32),
            pltpu.VMEM((W, W), F32),
            pltpu.VMEM((DEPTH, 2, W, W), F32),
            pltpu.VMEM((2, 2, BAND, OW), BF16),
            pltpu.VMEM((2, 2, BAND, OW), BF16),
            pltpu.VMEM((2, DEPTH, 2, BAND, W), BF16),
            pltpu.VMEM((2, DEPTH, 2, BAND, W), BF16),
            pltpu.VMEM((2, DEPTH, 2, BAND, W), BF16),
            pltpu.VMEM((2, DEPTH, 2, BAND, W), BF16),
            pltpu.VMEM((2, 2, BAND, OW), BF16),
            pltpu.VMEM((2, 2, BAND, OW), BF16),
            pltpu.VMEM((2, DEPTH, 2, BAND, W), BF16),
            pltpu.VMEM((2, DEPTH, 2, BAND, W), BF16),
            pltpu.VMEM((8, W), F32),
            pltpu.VMEM((2, 8, W), F32),
            pltpu.SMEM((2, DEPTH), jnp.int32),
            pltpu.SMEM((1, 2), jnp.int32),
            dma((8,)), dma((2, PARTS)), dma((2, PARTS)), dma((1 + PARTS, DEPTH)), dma((1 + PARTS, DEPTH)),
            dma((2, DEPTH)), dma((2, DEPTH)), dma((2,)), dma((2,)),
            dma((2, DEPTH)), dma((2, DEPTH)), dma((2,)), dma((2,)),
        ],
        compiler_params=pltpu.CompilerParams(collective_id=0, has_side_effects=True, vmem_limit_bytes=66506752),
    )(positions.T, extents, transmission, probe_wave, fresnel_phase, measured,
      jnp.asarray(right), jnp.asarray(left))


def solution(mesh):
    tile_count = mesh.shape["tile"]
    placed = (
        P(None, "depth", "tile", None),
        P(),
        P(),
        P("tile", None, None),
        P("tile", None),
        P("tile", None),
    )

    def body(*args):
        return shards(tile_count, *args)

    return jax.shard_map(
        body,
        mesh=mesh,
        in_specs=placed,
        out_specs=P(None, "depth", "tile", None),
        check_vma=False,
    )
```

```python
import math

import jax
import jax.numpy as jnp
import numpy as np
from jax import lax
from jax.experimental import pallas as pl
from jax.experimental.pallas import tpu as pltpu
from jax.sharding import PartitionSpec as P

BAND = 64
W = 128
STRIP = 128
OW = 512
BLOCKS = OW // W
DEPTH = 4
RUN = 16
PARTS = 2
LATER = (0, 1)
FORWARD = (3, 2)
TURN = (2, 2)
BACKWARD = (2, 2)
PART = BAND // PARTS
F32 = jnp.float32
BF16 = jnp.bfloat16
MESH = pl.DeviceIdType.MESH


def dft_matrices():
    index = np.arange(W)
    angles = (index[:, None] * index[None, :] % W) * (2.0 * math.pi / W)
    cosine = np.cos(angles) / math.sqrt(W)
    sine = np.sin(angles) / math.sqrt(W)
    a = np.block([[cosine, sine], [-sine, cosine]])
    b = a.T
    parts = []
    for m in (a, b):
        high = m.astype(BF16)
        low = (m - high.astype(np.float64)).astype(BF16)
        parts.append((high, low))
    right = np.stack([np.concatenate([h, l, h], axis=0) for h, l in (parts[1], parts[0])])
    left = np.stack([np.concatenate([h, l, h], axis=1) for h, l in (parts[0], parts[1])])
    return right, left


def kernel(
    tile_count,
    pos_hbm, ext_hbm, tr_hbm, probe_hbm, phase_hbm, meas_hbm, right_hbm, left_hbm,
    out_ref,
    tr, probe, phase, meas, right, left, gcos, gsin, waves,
    halo_send, halo, wsend, wrecv, gsend, grecv, band_send, band_recv, far_send, far_recv, col_send, col_recv, pos_ref, ext_ref,
    local_sem, hs, hr, ws, wr, gs, gr, bs, br, fs, fr, cs, cr,
):
    t = lax.axis_index("tile")
    me = lax.axis_index("depth")
    above = lax.rem(t + tile_count - 1, tile_count)
    below = lax.rem(t + 1, tile_count)
    peers = [lax.rem(me + j, DEPTH) for j in range(1, DEPTH)]

    sides = (above, below)

    def straight(tile):
        place = lax.rem(tile, RUN)
        return (place == 0) | (place == RUN - 1)

    out_straight = [straight(t)] * 2
    in_straight = [straight(side) for side in sides]
    even = lax.rem(lax.div(t, RUN), 2) == 0
    urgent = jnp.where((lax.rem(t, RUN) == 0) == even, 1, 0)

    barrier = pltpu.get_barrier_semaphore()
    for side in sides:
        pl.semaphore_signal(barrier, inc=1, device_id=(side, me), device_id_type=MESH)
    expected = 2 + len(peers)
    for i in range(2):
        for p in peers:
            wide = out_straight[i] | in_straight[i]
            expected = expected + jnp.where(wide, 1, 0)

            @pl.when(wide)
            def _():
                pl.semaphore_signal(barrier, inc=1, device_id=(sides[i], p), device_id_type=MESH)

    for p in peers:
        pl.semaphore_signal(barrier, inc=1, device_id=(t, p), device_id_type=MESH)

    fetches = [
        pltpu.make_async_copy(tr_hbm.at[:, 0], tr, local_sem.at[0]),
        pltpu.make_async_copy(probe_hbm, probe, local_sem.at[1]),
        pltpu.make_async_copy(phase_hbm, phase, local_sem.at[2]),
        pltpu.make_async_copy(meas_hbm.at[me], meas, local_sem.at[3]),
        pltpu.make_async_copy(right_hbm, right, local_sem.at[4]),
        pltpu.make_async_copy(left_hbm, left, local_sem.at[5]),
        pltpu.make_async_copy(pos_hbm, pos_ref, local_sem.at[6]),
        pltpu.make_async_copy(ext_hbm, ext_ref, local_sem.at[7]),
    ]
    for i in (6, 7, 0):
        fetches[i].start()
    for f in fetches[6:]:
        f.wait()

    def offset_of(p):
        rows = STRIP * tile_count
        return lax.rem(pos_ref[0, p] - t * STRIP + (rows + BAND), rows) - BAND

    offs = [offset_of(p) for p in range(DEPTH)]
    cols = [pos_ref[1, p] for p in range(DEPTH)]
    order = list(reversed(peers)) + [me]

    half_rows = lax.broadcasted_iota(jnp.int32, (BAND, W), 0)
    half_lanes = lax.broadcasted_iota(jnp.int32, (BAND, W), 1)

    def column_mask(p, m):
        position = half_lanes + m * W
        return (position >= cols[p]) & (position < cols[p] + W)

    def upward(p):
        return (half_rows * 0 + offs[p]) <= 0

    fetches[0].wait()
    for i in range(2):
        halo_send[i] = tr[:, i * BAND:(i + 1) * BAND, :].astype(BF16)

    which = lax.broadcasted_iota(jnp.int32, (8, W), 0)
    columns = which * 0
    for p in range(DEPTH):
        columns = jnp.where(which == p, cols[p], columns)
    col_send[...] = columns.astype(F32)

    pl.semaphore_wait(barrier, expected)

    def part_rows(q):
        return slice(q * PART, (q + 1) * PART)

    def halo_copy(i, q):
        return pltpu.make_async_remote_copy(
            src_ref=halo_send.at[i, :, part_rows(q)], dst_ref=halo.at[1 - i, :, part_rows(q)],
            send_sem=hs.at[i, q], recv_sem=hr.at[1 - i, q],
            device_id=(sides[i], me), device_id_type=MESH,
        )

    def window_part(ref, h, k):
        return ref.at[0, k] if h == 0 else ref.at[1, k, :, part_rows(h - 1)]

    def window_copy(h, p):
        return pltpu.make_async_remote_copy(
            src_ref=window_part(wsend, h, p), dst_ref=window_part(wrecv, h, me),
            send_sem=ws.at[h, p], recv_sem=wr.at[h, me],
            device_id=(t, p), device_id_type=MESH,
        )

    def window_arrival(h, k):
        return pltpu.make_async_remote_copy(
            src_ref=window_part(wsend, h, k), dst_ref=window_part(wrecv, h, k),
            send_sem=ws.at[h, k], recv_sem=wr.at[h, k],
            device_id=(t, k), device_id_type=MESH,
        )

    for q in range(PARTS):
        for i in range(2):
            halo_copy(i, q).start()
    for i in range(1, 6):
        fetches[i].start()

    def cut_masks(p):
        start = pos_ref[1, p]
        shift = offset_of(p)
        up = (half_rows * 0 + shift) <= 0
        outside = jnp.where(up, half_rows - (BAND + shift), shift - 1 - half_rows) >= 0
        lanes = [(half_lanes + m * W >= start) & (half_lanes + m * W < start + W) for m in range(BLOCKS)]
        return up, outside, lanes

    for p in order:
        up, _, picks = cut_masks(p)
        for c in range(2):
            total = jnp.zeros((BAND, W), F32)
            for m in range(BLOCKS):
                lanes = slice(m * W, (m + 1) * W)
                total = jnp.where(picks[m], jnp.where(up, tr[c, :BAND, lanes], tr[c, BAND:, lanes]), total)
            if p is me:
                wrecv[0, me, c] = total.astype(BF16)
            else:
                wsend[0, p, c] = total.astype(BF16)
        if p is not me:
            window_copy(0, p).start()

    def column_copy(i):
        return pltpu.make_async_remote_copy(
            src_ref=col_send, dst_ref=col_recv.at[1 - i],
            send_sem=cs.at[i], recv_sem=cr.at[1 - i],
            device_id=(sides[i], me), device_id_type=MESH,
        )

    for i in range(2):
        @pl.when(out_straight[i])
        def _():
            column_copy(i).start()

    fetches[2].wait()
    gcos[...] = jnp.cos(phase[...])
    gsin[...] = jnp.sin(phase[...])
    my_off = offset_of(me)
    my_col = pos_ref[1, me]
    rows = lax.broadcasted_iota(jnp.int32, (W, W), 0)
    extended = my_off + ((rows - my_off + W) & (W - 1))
    inside = (extended >= -ext_ref[0, 0]) & (extended < STRIP + ext_ref[0, 1])
    fetches[1].wait()
    for c in range(2):
        turned = pltpu.roll(probe[c], (my_off + W) & (W - 1), 0)
        turned = pltpu.roll(turned, my_col & (W - 1), 1)
        waves[0, c] = jnp.where(inside, turned, 0.0)

    for q in range(PARTS):
        for i in range(2):
            halo_copy(i, q).wait_recv()
        for p in order:
            up, outside, picks = cut_masks(p)
            up, outside = up[part_rows(q)], outside[part_rows(q)]
            for c in range(2):
                total = jnp.zeros((PART, W), F32)
                for m in range(BLOCKS):
                    lanes = slice(m * W, (m + 1) * W)
                    outer = jnp.where(up, halo[0, c, part_rows(q), lanes].astype(F32), halo[1, c, part_rows(q), lanes].astype(F32))
                    inner = jnp.where(up, tr[c, BAND + q * PART:BAND + (q + 1) * PART, lanes], tr[c, part_rows(q), lanes])
                    total = jnp.where(picks[m][part_rows(q)], jnp.where(outside, outer, inner), total)
                if p is me:
                    wrecv[1, me, c, part_rows(q)] = total.astype(BF16)
                else:
                    wsend[1, p, c, part_rows(q)] = total.astype(BF16)
            if p is not me:
                window_copy(q + 1, p).start()

    for i in (3, 4, 5):
        fetches[i].wait()

    up_me = (half_rows * 0 + my_off) <= 0

    def layer(k):
        both = []
        for c in range(2):
            certain = wrecv[0, k, c].astype(F32)
            mixed = wrecv[1, k, c].astype(F32)
            both.append(jnp.concatenate(
                [jnp.where(up_me, certain, mixed), jnp.where(up_me, mixed, certain)], axis=0))
        return both

    def parts_of(x, products):
        high = x.astype(BF16)
        parts = [high] * min(products, 2)
        if products == 3:
            parts.append((x - high.astype(F32)).astype(BF16))
        return parts

    def transform(re, im, inverse, products):
        d = 1 if inverse else 0
        n_right, n_left = products
        x = jnp.concatenate([re, im], axis=1)
        u = jnp.dot(jnp.concatenate(parts_of(x, n_right), axis=1), right[d, :n_right * 2 * W, :],
                    preferred_element_type=F32)
        x = jnp.concatenate([u[:, :W], u[:, W:]], axis=0)
        v = jnp.dot(left[d, :, :n_left * 2 * W], jnp.concatenate(parts_of(x, n_left), axis=0),
                    preferred_element_type=F32)
        return v[:W], v[W:]

    def propagate(re, im, conjugate, products):
        re, im = transform(re, im, False, products)
        co, si = gcos[...], gsin[...]
        if conjugate:
            re, im = re * co + im * si, im * co - re * si
        else:
            re, im = re * co - im * si, im * co + re * si
        return transform(re, im, True, products)

    re = im = None
    for k in range(DEPTH):
        for h in range(1 + PARTS):
            @pl.when(me != k)
            def _():
                window_arrival(h, k).wait_recv()
        o_re, o_im = layer(k)
        if k == 0:
            re, im = waves[0, 0], waves[0, 1]
        else:
            waves[k, 0] = re
            waves[k, 1] = im
        re, im = re * o_re - im * o_im, re * o_im + im * o_re
        if k + 1 < DEPTH:
            re, im = propagate(re, im, False, FORWARD)
    re, im = transform(re, im, False, FORWARD)
    misfit = re * re + im * im - meas[...]
    re, im = transform(misfit * re, misfit * im, True, TURN)

    from_halo_me = jnp.where(up_me, half_rows - (BAND + my_off), my_off - 1 - half_rows) >= 0

    def gradient_copy(k, h):
        return pltpu.make_async_remote_copy(
            src_ref=gsend.at[h, k], dst_ref=grecv.at[h, me],
            send_sem=gs.at[h, k], recv_sem=gr.at[h, me],
            device_id=(t, k), device_id_type=MESH,
        )

    def far_copy(i, k):
        return pltpu.make_async_remote_copy(
            src_ref=far_send.at[i, k], dst_ref=far_recv.at[1 - i, me],
            send_sem=fs.at[i, k], recv_sem=fr.at[1 - i, me],
            device_id=(jnp.where(i == 0, above, below), k), device_id_type=MESH,
        )

    def far_arrival(i, p):
        return pltpu.make_async_remote_copy(
            src_ref=far_send.at[i, p], dst_ref=far_recv.at[i, p],
            send_sem=fs.at[i, p], recv_sem=fr.at[i, p],
            device_id=(sides[i], p), device_id_type=MESH,
        )

    def gradient_arrival(p, h):
        return pltpu.make_async_remote_copy(
            src_ref=gsend.at[h, p], dst_ref=grecv.at[h, p],
            send_sem=gs.at[h, p], recv_sem=gr.at[h, p],
            device_id=(t, p), device_id_type=MESH,
        )

    for k in reversed(range(DEPTH)):
        if k + 1 < DEPTH:
            re, im = propagate(re, im, True, BACKWARD)
        w_re, w_im = waves[k, 0], waves[k, 1]
        terms = (w_re * re + w_im * im, w_re * im - w_im * re)

        @pl.when(straight(t))
        def _():
            for c in range(2):
                mixed = jnp.where(up_me, terms[c][BAND:], terms[c][:BAND])
                mixed = jnp.where(from_halo_me, mixed, 0.0)
                far_send[0, k, c] = jnp.where(up_me, mixed, 0.0).astype(BF16)
                far_send[1, k, c] = jnp.where(up_me, 0.0, mixed).astype(BF16)
            far_copy(urgent, k).start()

        for c in range(2):
            lower, upper = terms[c][:BAND], terms[c][BAND:]
            gsend[1, k, c] = jnp.where(up_me, upper, lower).astype(BF16)
            gsend[0, k, c] = jnp.where(up_me, lower, upper).astype(BF16)

        @pl.when(me != k)
        def _():
            gradient_copy(k, 1).start()
            if k not in LATER:
                gradient_copy(k, 0).start()

        @pl.when(straight(t))
        def _():
            far_copy(1 - urgent, k).start()

        @pl.when(me == k)
        def _():
            grecv[1, me] = gsend[1, k]
            grecv[0, me] = gsend[0, k]

        if k > 0:
            o_re, o_im = layer(k)
            re, im = o_re * re + o_im * im, o_re * im - o_im * re

    for k in LATER:
        @pl.when(me != k)
        def _():
            gradient_copy(k, 0).start()

    for p in peers:
        gradient_arrival(p, 1).wait_recv()
    def band_copy(i):
        return pltpu.make_async_remote_copy(
            src_ref=band_send.at[i], dst_ref=band_recv.at[1 - i],
            send_sem=bs.at[i], recv_sem=br.at[1 - i],
            device_id=(above if i == 0 else below, me), device_id_type=MESH,
        )

    for c in range(2):
        for m in range(BLOCKS):
            lanes = slice(m * W, (m + 1) * W)
            top = bottom = jnp.zeros((BAND, W), F32)
            for p in range(DEPTH):
                up = upward(p)
                from_halo = jnp.where(up, half_rows - (BAND + offs[p]), offs[p] - 1 - half_rows) >= 0
                piece = jnp.where(from_halo & column_mask(p, m), grecv[1, p, c].astype(F32), 0.0)
                top = top + jnp.where(up, piece, 0.0)
                bottom = bottom + jnp.where(up, 0.0, piece)
            band_send[0, c, :, lanes] = top.astype(BF16)
            band_send[1, c, :, lanes] = bottom.astype(BF16)
    for i in range(2):
        @pl.when(~out_straight[i])
        def _():
            band_copy(i).start()

    for p in peers:
        gradient_arrival(p, 0).wait_recv()
    for c in range(2):
        for m in range(BLOCKS):
            lanes = slice(m * W, (m + 1) * W)
            top = bottom = jnp.zeros((BAND, W), F32)
            for p in range(DEPTH):
                up = upward(p)
                from_halo = jnp.where(up, half_rows - (BAND + offs[p]), offs[p] - 1 - half_rows) >= 0
                mask = column_mask(p, m)
                certain = jnp.where(mask, grecv[0, p, c].astype(F32), 0.0)
                mixed = jnp.where(mask & ~from_halo, grecv[1, p, c].astype(F32), 0.0)
                top = top + jnp.where(up, certain, mixed)
                bottom = bottom + jnp.where(up, mixed, certain)
            out_ref[c, 0, :BAND, lanes] = top
            out_ref[c, 0, BAND:, lanes] = bottom
    lanes_f = half_lanes.astype(F32)
    for i in range(2):
        edge = slice(i * BAND, (i + 1) * BAND)

        @pl.when(~in_straight[i])
        def _():
            band_copy(1 - i).wait_recv()
            out_ref[:, 0, edge, :] = out_ref[:, 0, edge, :] + band_recv[i].astype(F32)

        @pl.when(in_straight[i])
        def _():
            column_copy(1 - i).wait_recv()
            for p in range(DEPTH):
                far_arrival(i, p).wait_recv()
            for m in range(BLOCKS):
                lanes = slice(m * W, (m + 1) * W)
                totals = [out_ref[c, 0, edge, lanes] for c in range(2)]
                for p in range(DEPTH):
                    start = col_recv[i, p:p + 1, :] - float(m * W)
                    mask = (lanes_f >= start) & (lanes_f < start + float(W))
                    for c in range(2):
                        totals[c] = totals[c] + jnp.where(mask, far_recv[i, p, c].astype(F32), 0.0)
                for c in range(2):
                    out_ref[c, 0, edge, lanes] = totals[c]

    for i in range(2):
        @pl.when(~out_straight[i])
        def _():
            band_copy(i).wait_send()

        @pl.when(out_straight[i])
        def _():
            column_copy(i).wait_send()

        for k in range(DEPTH):
            @pl.when(out_straight[i])
            def _():
                far_copy(i, k).wait_send()

    for i in range(2):
        for q in range(PARTS):
            halo_copy(i, q).wait_send()
    for p in peers:
        for h in range(1 + PARTS):
            window_copy(h, p).wait_send()
        for h in range(2):
            gradient_copy(p, h).wait_send()


def shards(tile_count, transmission, probe_wave, fresnel_phase, measured, positions, extents):
    right, left = dft_matrices()
    any_spec = pl.BlockSpec(memory_space=pl.ANY)
    dma = pltpu.SemaphoreType.DMA

    def body(*refs):
        kernel(tile_count, *refs)

    return pl.pallas_call(
        body,
        out_shape=pltpu.VMEM(transmission.shape, F32),
        in_specs=[any_spec] * 8,
        out_specs=pl.BlockSpec(memory_space=pltpu.VMEM),
        scratch_shapes=[
            pltpu.VMEM((2, STRIP, OW), F32),
            pltpu.VMEM((2, W, W), F32),
            pltpu.VMEM((W, W), F32),
            pltpu.VMEM((W, W), F32),
            pltpu.VMEM(right.shape, BF16),
            pltpu.VMEM(left.shape, BF16),
            pltpu.VMEM((W, W), F32),
            pltpu.VMEM((W, W), F32),
            pltpu.VMEM((DEPTH, 2, W, W), F32),
            pltpu.VMEM((2, 2, BAND, OW), BF16),
            pltpu.VMEM((2, 2, BAND, OW), BF16),
            pltpu.VMEM((2, DEPTH, 2, BAND, W), BF16),
            pltpu.VMEM((2, DEPTH, 2, BAND, W), BF16),
            pltpu.VMEM((2, DEPTH, 2, BAND, W), BF16),
            pltpu.VMEM((2, DEPTH, 2, BAND, W), BF16),
            pltpu.VMEM((2, 2, BAND, OW), BF16),
            pltpu.VMEM((2, 2, BAND, OW), BF16),
            pltpu.VMEM((2, DEPTH, 2, BAND, W), BF16),
            pltpu.VMEM((2, DEPTH, 2, BAND, W), BF16),
            pltpu.VMEM((8, W), F32),
            pltpu.VMEM((2, 8, W), F32),
            pltpu.SMEM((2, DEPTH), jnp.int32),
            pltpu.SMEM((1, 2), jnp.int32),
            dma((8,)), dma((2, PARTS)), dma((2, PARTS)), dma((1 + PARTS, DEPTH)), dma((1 + PARTS, DEPTH)),
            dma((2, DEPTH)), dma((2, DEPTH)), dma((2,)), dma((2,)),
            dma((2, DEPTH)), dma((2, DEPTH)), dma((2,)), dma((2,)),
        ],
        compiler_params=pltpu.CompilerParams(collective_id=0, has_side_effects=True, vmem_limit_bytes=66506752),
    )(positions.T, extents, transmission, probe_wave, fresnel_phase, measured,
      jnp.asarray(right), jnp.asarray(left))


def solution(mesh):
    tile_count = mesh.shape["tile"]
    placed = (
        P(None, "depth", "tile", None),
        P(),
        P(),
        P("tile", None, None),
        P("tile", None),
        P("tile", None),
    )

    def body(*args):
        return shards(tile_count, *args)

    return jax.shard_map(
        body,
        mesh=mesh,
        in_specs=placed,
        out_specs=P(None, "depth", "tile", None),
        check_vma=False,
    )
```

```python
import math

import jax
import jax.numpy as jnp
import numpy as np
from jax import lax
from jax.experimental import pallas as pl
from jax.experimental.pallas import tpu as pltpu
from jax.sharding import PartitionSpec as P

BAND = 64
W = 128
STRIP = 128
OW = 512
BLOCKS = OW // W
DEPTH = 4
RUN = 16
PARTS = 2
LATER = (0, 1, 2)
FORWARD = (3, 2)
TURN = (2, 2)
BACKWARD = (2, 2)
PART = BAND // PARTS
F32 = jnp.float32
BF16 = jnp.bfloat16
MESH = pl.DeviceIdType.MESH


def dft_matrices():
    index = np.arange(W)
    angles = (index[:, None] * index[None, :] % W) * (2.0 * math.pi / W)
    cosine = np.cos(angles) / math.sqrt(W)
    sine = np.sin(angles) / math.sqrt(W)
    a = np.block([[cosine, sine], [-sine, cosine]])
    b = a.T
    parts = []
    for m in (a, b):
        high = m.astype(BF16)
        low = (m - high.astype(np.float64)).astype(BF16)
        parts.append((high, low))
    right = np.stack([np.concatenate([h, l, h], axis=0) for h, l in (parts[1], parts[0])])
    left = np.stack([np.concatenate([h, l, h], axis=1) for h, l in (parts[0], parts[1])])
    return right, left


def kernel(
    tile_count,
    pos_hbm, ext_hbm, tr_hbm, probe_hbm, phase_hbm, meas_hbm, right_hbm, left_hbm,
    out_ref,
    tr, probe, phase, meas, right, left, gcos, gsin, waves,
    halo_send, halo, wsend, wrecv, gsend, grecv, band_send, band_recv, far_send, far_recv, col_send, col_recv, pos_ref, ext_ref,
    local_sem, hs, hr, ws, wr, gs, gr, bs, br, fs, fr, cs, cr,
):
    t = lax.axis_index("tile")
    me = lax.axis_index("depth")
    above = lax.rem(t + tile_count - 1, tile_count)
    below = lax.rem(t + 1, tile_count)
    peers = [lax.rem(me + j, DEPTH) for j in range(1, DEPTH)]

    sides = (above, below)

    def straight(tile):
        place = lax.rem(tile, RUN)
        return (place == 0) | (place == RUN - 1)

    out_straight = [straight(t)] * 2
    in_straight = [straight(side) for side in sides]
    even = lax.rem(lax.div(t, RUN), 2) == 0
    urgent = jnp.where((lax.rem(t, RUN) == 0) == even, 1, 0)

    barrier = pltpu.get_barrier_semaphore()
    for side in sides:
        pl.semaphore_signal(barrier, inc=1, device_id=(side, me), device_id_type=MESH)
    expected = 2 + len(peers)
    for i in range(2):
        for p in peers:
            wide = out_straight[i] | in_straight[i]
            expected = expected + jnp.where(wide, 1, 0)

            @pl.when(wide)
            def _():
                pl.semaphore_signal(barrier, inc=1, device_id=(sides[i], p), device_id_type=MESH)

    for p in peers:
        pl.semaphore_signal(barrier, inc=1, device_id=(t, p), device_id_type=MESH)

    fetches = [
        pltpu.make_async_copy(tr_hbm.at[:, 0], tr, local_sem.at[0]),
        pltpu.make_async_copy(probe_hbm, probe, local_sem.at[1]),
        pltpu.make_async_copy(phase_hbm, phase, local_sem.at[2]),
        pltpu.make_async_copy(meas_hbm.at[me], meas, local_sem.at[3]),
        pltpu.make_async_copy(right_hbm, right, local_sem.at[4]),
        pltpu.make_async_copy(left_hbm, left, local_sem.at[5]),
        pltpu.make_async_copy(pos_hbm, pos_ref, local_sem.at[6]),
        pltpu.make_async_copy(ext_hbm, ext_ref, local_sem.at[7]),
    ]
    for i in (6, 7, 0):
        fetches[i].start()
    for f in fetches[6:]:
        f.wait()

    def offset_of(p):
        rows = STRIP * tile_count
        return lax.rem(pos_ref[0, p] - t * STRIP + (rows + BAND), rows) - BAND

    offs = [offset_of(p) for p in range(DEPTH)]
    cols = [pos_ref[1, p] for p in range(DEPTH)]
    order = list(reversed(peers)) + [me]

    half_rows = lax.broadcasted_iota(jnp.int32, (BAND, W), 0)
    half_lanes = lax.broadcasted_iota(jnp.int32, (BAND, W), 1)

    def column_mask(p, m):
        position = half_lanes + m * W
        return (position >= cols[p]) & (position < cols[p] + W)

    def upward(p):
        return (half_rows * 0 + offs[p]) <= 0

    fetches[0].wait()
    for i in range(2):
        halo_send[i] = tr[:, i * BAND:(i + 1) * BAND, :].astype(BF16)

    which = lax.broadcasted_iota(jnp.int32, (8, W), 0)
    columns = which * 0
    for p in range(DEPTH):
        columns = jnp.where(which == p, cols[p], columns)
    col_send[...] = columns.astype(F32)

    pl.semaphore_wait(barrier, expected)

    def part_rows(q):
        return slice(q * PART, (q + 1) * PART)

    def halo_copy(i, q):
        return pltpu.make_async_remote_copy(
            src_ref=halo_send.at[i, :, part_rows(q)], dst_ref=halo.at[1 - i, :, part_rows(q)],
            send_sem=hs.at[i, q], recv_sem=hr.at[1 - i, q],
            device_id=(sides[i], me), device_id_type=MESH,
        )

    def window_part(ref, h, k):
        return ref.at[0, k] if h == 0 else ref.at[1, k, :, part_rows(h - 1)]

    def window_copy(h, p):
        return pltpu.make_async_remote_copy(
            src_ref=window_part(wsend, h, p), dst_ref=window_part(wrecv, h, me),
            send_sem=ws.at[h, p], recv_sem=wr.at[h, me],
            device_id=(t, p), device_id_type=MESH,
        )

    def window_arrival(h, k):
        return pltpu.make_async_remote_copy(
            src_ref=window_part(wsend, h, k), dst_ref=window_part(wrecv, h, k),
            send_sem=ws.at[h, k], recv_sem=wr.at[h, k],
            device_id=(t, k), device_id_type=MESH,
        )

    for q in range(PARTS):
        for i in range(2):
            halo_copy(i, q).start()
    for i in range(1, 6):
        fetches[i].start()

    def cut_masks(p):
        start = pos_ref[1, p]
        shift = offset_of(p)
        up = (half_rows * 0 + shift) <= 0
        outside = jnp.where(up, half_rows - (BAND + shift), shift - 1 - half_rows) >= 0
        lanes = [(half_lanes + m * W >= start) & (half_lanes + m * W < start + W) for m in range(BLOCKS)]
        return up, outside, lanes

    for p in order:
        up, _, picks = cut_masks(p)
        for c in range(2):
            total = jnp.zeros((BAND, W), F32)
            for m in range(BLOCKS):
                lanes = slice(m * W, (m + 1) * W)
                total = jnp.where(picks[m], jnp.where(up, tr[c, :BAND, lanes], tr[c, BAND:, lanes]), total)
            if p is me:
                wrecv[0, me, c] = total.astype(BF16)
            else:
                wsend[0, p, c] = total.astype(BF16)
        if p is not me:
            window_copy(0, p).start()

    def column_copy(i):
        return pltpu.make_async_remote_copy(
            src_ref=col_send, dst_ref=col_recv.at[1 - i],
            send_sem=cs.at[i], recv_sem=cr.at[1 - i],
            device_id=(sides[i], me), device_id_type=MESH,
        )

    for i in range(2):
        @pl.when(out_straight[i])
        def _():
            column_copy(i).start()

    fetches[2].wait()
    gcos[...] = jnp.cos(phase[...])
    gsin[...] = jnp.sin(phase[...])
    my_off = offset_of(me)
    my_col = pos_ref[1, me]
    rows = lax.broadcasted_iota(jnp.int32, (W, W), 0)
    extended = my_off + ((rows - my_off + W) & (W - 1))
    inside = (extended >= -ext_ref[0, 0]) & (extended < STRIP + ext_ref[0, 1])
    fetches[1].wait()
    for c in range(2):
        turned = pltpu.roll(probe[c], (my_off + W) & (W - 1), 0)
        turned = pltpu.roll(turned, my_col & (W - 1), 1)
        waves[0, c] = jnp.where(inside, turned, 0.0)

    for q in range(PARTS):
        for i in range(2):
            halo_copy(i, q).wait_recv()
        for p in order:
            up, outside, picks = cut_masks(p)
            up, outside = up[part_rows(q)], outside[part_rows(q)]
            for c in range(2):
                total = jnp.zeros((PART, W), F32)
                for m in range(BLOCKS):
                    lanes = slice(m * W, (m + 1) * W)
                    outer = jnp.where(up, halo[0, c, part_rows(q), lanes].astype(F32), halo[1, c, part_rows(q), lanes].astype(F32))
                    inner = jnp.where(up, tr[c, BAND + q * PART:BAND + (q + 1) * PART, lanes], tr[c, part_rows(q), lanes])
                    total = jnp.where(picks[m][part_rows(q)], jnp.where(outside, outer, inner), total)
                if p is me:
                    wrecv[1, me, c, part_rows(q)] = total.astype(BF16)
                else:
                    wsend[1, p, c, part_rows(q)] = total.astype(BF16)
            if p is not me:
                window_copy(q + 1, p).start()

    for i in (3, 4, 5):
        fetches[i].wait()

    up_me = (half_rows * 0 + my_off) <= 0

    def layer(k):
        both = []
        for c in range(2):
            certain = wrecv[0, k, c].astype(F32)
            mixed = wrecv[1, k, c].astype(F32)
            both.append(jnp.concatenate(
                [jnp.where(up_me, certain, mixed), jnp.where(up_me, mixed, certain)], axis=0))
        return both

    def parts_of(x, products):
        high = x.astype(BF16)
        parts = [high] * min(products, 2)
        if products == 3:
            parts.append((x - high.astype(F32)).astype(BF16))
        return parts

    def transform(re, im, inverse, products):
        d = 1 if inverse else 0
        n_right, n_left = products
        x = jnp.concatenate([re, im], axis=1)
        u = jnp.dot(jnp.concatenate(parts_of(x, n_right), axis=1), right[d, :n_right * 2 * W, :],
                    preferred_element_type=F32)
        x = jnp.concatenate([u[:, :W], u[:, W:]], axis=0)
        v = jnp.dot(left[d, :, :n_left * 2 * W], jnp.concatenate(parts_of(x, n_left), axis=0),
                    preferred_element_type=F32)
        return v[:W], v[W:]

    def propagate(re, im, conjugate, products):
        re, im = transform(re, im, False, products)
        co, si = gcos[...], gsin[...]
        if conjugate:
            re, im = re * co + im * si, im * co - re * si
        else:
            re, im = re * co - im * si, im * co + re * si
        return transform(re, im, True, products)

    re = im = None
    for k in range(DEPTH):
        for h in range(1 + PARTS):
            @pl.when(me != k)
            def _():
                window_arrival(h, k).wait_recv()
        o_re, o_im = layer(k)
        if k == 0:
            re, im = waves[0, 0], waves[0, 1]
        else:
            waves[k, 0] = re
            waves[k, 1] = im
        re, im = re * o_re - im * o_im, re * o_im + im * o_re
        if k + 1 < DEPTH:
            re, im = propagate(re, im, False, FORWARD)
    re, im = transform(re, im, False, FORWARD)
    misfit = re * re + im * im - meas[...]
    re, im = transform(misfit * re, misfit * im, True, TURN)

    from_halo_me = jnp.where(up_me, half_rows - (BAND + my_off), my_off - 1 - half_rows) >= 0

    def gradient_copy(k, h):
        return pltpu.make_async_remote_copy(
            src_ref=gsend.at[h, k], dst_ref=grecv.at[h, me],
            send_sem=gs.at[h, k], recv_sem=gr.at[h, me],
            device_id=(t, k), device_id_type=MESH,
        )

    def far_copy(i, k):
        return pltpu.make_async_remote_copy(
            src_ref=far_send.at[i, k], dst_ref=far_recv.at[1 - i, me],
            send_sem=fs.at[i, k], recv_sem=fr.at[1 - i, me],
            device_id=(jnp.where(i == 0, above, below), k), device_id_type=MESH,
        )

    def far_arrival(i, p):
        return pltpu.make_async_remote_copy(
            src_ref=far_send.at[i, p], dst_ref=far_recv.at[i, p],
            send_sem=fs.at[i, p], recv_sem=fr.at[i, p],
            device_id=(sides[i], p), device_id_type=MESH,
        )

    def gradient_arrival(p, h):
        return pltpu.make_async_remote_copy(
            src_ref=gsend.at[h, p], dst_ref=grecv.at[h, p],
            send_sem=gs.at[h, p], recv_sem=gr.at[h, p],
            device_id=(t, p), device_id_type=MESH,
        )

    for k in reversed(range(DEPTH)):
        if k + 1 < DEPTH:
            re, im = propagate(re, im, True, BACKWARD)
        w_re, w_im = waves[k, 0], waves[k, 1]
        terms = (w_re * re + w_im * im, w_re * im - w_im * re)

        @pl.when(straight(t))
        def _():
            for c in range(2):
                mixed = jnp.where(up_me, terms[c][BAND:], terms[c][:BAND])
                mixed = jnp.where(from_halo_me, mixed, 0.0)
                far_send[0, k, c] = jnp.where(up_me, mixed, 0.0).astype(BF16)
                far_send[1, k, c] = jnp.where(up_me, 0.0, mixed).astype(BF16)
            far_copy(urgent, k).start()

        for c in range(2):
            lower, upper = terms[c][:BAND], terms[c][BAND:]
            gsend[1, k, c] = jnp.where(up_me, upper, lower).astype(BF16)
            gsend[0, k, c] = jnp.where(up_me, lower, upper).astype(BF16)

        @pl.when(me != k)
        def _():
            gradient_copy(k, 1).start()
            if k not in LATER:
                gradient_copy(k, 0).start()

        @pl.when(straight(t))
        def _():
            far_copy(1 - urgent, k).start()

        @pl.when(me == k)
        def _():
            grecv[1, me] = gsend[1, k]
            grecv[0, me] = gsend[0, k]

        if k > 0:
            o_re, o_im = layer(k)
            re, im = o_re * re + o_im * im, o_re * im - o_im * re

    for k in LATER:
        @pl.when(me != k)
        def _():
            gradient_copy(k, 0).start()

    for p in peers:
        gradient_arrival(p, 1).wait_recv()
    def band_copy(i):
        return pltpu.make_async_remote_copy(
            src_ref=band_send.at[i], dst_ref=band_recv.at[1 - i],
            send_sem=bs.at[i], recv_sem=br.at[1 - i],
            device_id=(above if i == 0 else below, me), device_id_type=MESH,
        )

    for c in range(2):
        for m in range(BLOCKS):
            lanes = slice(m * W, (m + 1) * W)
            top = bottom = jnp.zeros((BAND, W), F32)
            for p in range(DEPTH):
                up = upward(p)
                from_halo = jnp.where(up, half_rows - (BAND + offs[p]), offs[p] - 1 - half_rows) >= 0
                piece = jnp.where(from_halo & column_mask(p, m), grecv[1, p, c].astype(F32), 0.0)
                top = top + jnp.where(up, piece, 0.0)
                bottom = bottom + jnp.where(up, 0.0, piece)
            band_send[0, c, :, lanes] = top.astype(BF16)
            band_send[1, c, :, lanes] = bottom.astype(BF16)
    for i in range(2):
        @pl.when(~out_straight[i])
        def _():
            band_copy(i).start()

    for p in peers:
        gradient_arrival(p, 0).wait_recv()
    for c in range(2):
        for m in range(BLOCKS):
            lanes = slice(m * W, (m + 1) * W)
            top = bottom = jnp.zeros((BAND, W), F32)
            for p in range(DEPTH):
                up = upward(p)
                from_halo = jnp.where(up, half_rows - (BAND + offs[p]), offs[p] - 1 - half_rows) >= 0
                mask = column_mask(p, m)
                certain = jnp.where(mask, grecv[0, p, c].astype(F32), 0.0)
                mixed = jnp.where(mask & ~from_halo, grecv[1, p, c].astype(F32), 0.0)
                top = top + jnp.where(up, certain, mixed)
                bottom = bottom + jnp.where(up, mixed, certain)
            out_ref[c, 0, :BAND, lanes] = top
            out_ref[c, 0, BAND:, lanes] = bottom
    lanes_f = half_lanes.astype(F32)
    for i in range(2):
        edge = slice(i * BAND, (i + 1) * BAND)

        @pl.when(~in_straight[i])
        def _():
            band_copy(1 - i).wait_recv()
            out_ref[:, 0, edge, :] = out_ref[:, 0, edge, :] + band_recv[i].astype(F32)

        @pl.when(in_straight[i])
        def _():
            column_copy(1 - i).wait_recv()
            for p in range(DEPTH):
                far_arrival(i, p).wait_recv()
            for m in range(BLOCKS):
                lanes = slice(m * W, (m + 1) * W)
                totals = [out_ref[c, 0, edge, lanes] for c in range(2)]
                for p in range(DEPTH):
                    start = col_recv[i, p:p + 1, :] - float(m * W)
                    mask = (lanes_f >= start) & (lanes_f < start + float(W))
                    for c in range(2):
                        totals[c] = totals[c] + jnp.where(mask, far_recv[i, p, c].astype(F32), 0.0)
                for c in range(2):
                    out_ref[c, 0, edge, lanes] = totals[c]

    for i in range(2):
        @pl.when(~out_straight[i])
        def _():
            band_copy(i).wait_send()

        @pl.when(out_straight[i])
        def _():
            column_copy(i).wait_send()

        for k in range(DEPTH):
            @pl.when(out_straight[i])
            def _():
                far_copy(i, k).wait_send()

    for i in range(2):
        for q in range(PARTS):
            halo_copy(i, q).wait_send()
    for p in peers:
        for h in range(1 + PARTS):
            window_copy(h, p).wait_send()
        for h in range(2):
            gradient_copy(p, h).wait_send()


def shards(tile_count, transmission, probe_wave, fresnel_phase, measured, positions, extents):
    right, left = dft_matrices()
    any_spec = pl.BlockSpec(memory_space=pl.ANY)
    dma = pltpu.SemaphoreType.DMA

    def body(*refs):
        kernel(tile_count, *refs)

    return pl.pallas_call(
        body,
        out_shape=pltpu.VMEM(transmission.shape, F32),
        in_specs=[any_spec] * 8,
        out_specs=pl.BlockSpec(memory_space=pltpu.VMEM),
        scratch_shapes=[
            pltpu.VMEM((2, STRIP, OW), F32),
            pltpu.VMEM((2, W, W), F32),
            pltpu.VMEM((W, W), F32),
            pltpu.VMEM((W, W), F32),
            pltpu.VMEM(right.shape, BF16),
            pltpu.VMEM(left.shape, BF16),
            pltpu.VMEM((W, W), F32),
            pltpu.VMEM((W, W), F32),
            pltpu.VMEM((DEPTH, 2, W, W), F32),
            pltpu.VMEM((2, 2, BAND, OW), BF16),
            pltpu.VMEM((2, 2, BAND, OW), BF16),
            pltpu.VMEM((2, DEPTH, 2, BAND, W), BF16),
            pltpu.VMEM((2, DEPTH, 2, BAND, W), BF16),
            pltpu.VMEM((2, DEPTH, 2, BAND, W), BF16),
            pltpu.VMEM((2, DEPTH, 2, BAND, W), BF16),
            pltpu.VMEM((2, 2, BAND, OW), BF16),
            pltpu.VMEM((2, 2, BAND, OW), BF16),
            pltpu.VMEM((2, DEPTH, 2, BAND, W), BF16),
            pltpu.VMEM((2, DEPTH, 2, BAND, W), BF16),
            pltpu.VMEM((8, W), F32),
            pltpu.VMEM((2, 8, W), F32),
            pltpu.SMEM((2, DEPTH), jnp.int32),
            pltpu.SMEM((1, 2), jnp.int32),
            dma((8,)), dma((2, PARTS)), dma((2, PARTS)), dma((1 + PARTS, DEPTH)), dma((1 + PARTS, DEPTH)),
            dma((2, DEPTH)), dma((2, DEPTH)), dma((2,)), dma((2,)),
            dma((2, DEPTH)), dma((2, DEPTH)), dma((2,)), dma((2,)),
        ],
        compiler_params=pltpu.CompilerParams(collective_id=0, has_side_effects=True, vmem_limit_bytes=66506752),
    )(positions.T, extents, transmission, probe_wave, fresnel_phase, measured,
      jnp.asarray(right), jnp.asarray(left))


def solution(mesh):
    tile_count = mesh.shape["tile"]
    placed = (
        P(None, "depth", "tile", None),
        P(),
        P(),
        P("tile", None, None),
        P("tile", None),
        P("tile", None),
    )

    def body(*args):
        return shards(tile_count, *args)

    return jax.shard_map(
        body,
        mesh=mesh,
        in_specs=placed,
        out_specs=P(None, "depth", "tile", None),
        check_vma=False,
    )
```
